256 devices in a mesh: shard: 32 (over y, z), cent: 8 (over x, core).
Axes of the slice: x: 4, y: 4, z: 8, core: 2. Of those that a mesh axis runs over, the one named last changes fastest.
Arguments:
- queries: bfloat16 [512, 32, 128], P('shard'), may hold values from -0.5 to 0.5
- centroids: bfloat16 [262144, 128], P('cent'), may hold values from -0.5 to 0.5
- passage_tokens: bfloat16 [3072, 128, 128], P('shard'), may hold values from -0.5 to 0.5
- live_token_count: int32 [3072], P('shard'), may hold values from 1 to 128
- passage_home: int32 [3072], replicated, may hold values from 0 to 3071, as said below
- candidates: int32 [512, 256], P('shard', 'cent'), may hold values from 0 to 3071, as said below
Outputs:
- probe_scores: float32 [512, 32, 4], P('shard')
- passage_scores: float32 [512, 256], P('shard', 'cent')
The draws below stay inside these ranges and needn't reach their ends.
Inputs may be any that keep to these rules, and one draw needn't show every extreme that they name: Every passage id appears once; passage p is stored in row passage_home[p], which shard passage_home[p] // 96 holds. Among the candidates of one device (its 16 queries times its 32 columns), at most 32 are stored on any one shard. Ids may repeat.
All inputs are finite; a program needn't handle non-finite values.
Results may differ from the reference program's by a relative error of at most 0.0003.
Values may be sent and summed in bfloat16 or wider, within the bound.
No kernel may reach another device: no remote copies, remote signals or barrier semaphores. Data moves between devices by JAX's collectives and lax.ppermute only.
A program may use at most 128 MiB of HBM per device.

```python
import jax
import jax.numpy as jnp
from jax import lax

DIM = 128
QT = 32
BLK = 128
CENT = 262144
NPROBE = 4
NCAND = 256
Q_DEV = 16
P_LOC = 96
NQ = 512
NPASS = 3072
CPD = 32
CAP = 32


def index_tables(key):
    shard_count = NPASS // P_LOC
    cent_count = NCAND // CPD
    home = jax.random.permutation(jax.random.fold_in(key, 11), NPASS).astype(jnp.int32)
    inverse = jnp.argsort(home).astype(jnp.int32)
    pair_count = Q_DEV * CPD
    slot_total = shard_count * CAP
    block_count = shard_count * cent_count
    hot_shard = jax.random.randint(jax.random.fold_in(key, 12), (), 0, shard_count)
    shard_bias = jax.random.randint(jax.random.fold_in(key, 13), (shard_count,), 0, 4096)
    slot_home = jnp.arange(slot_total, dtype=jnp.int32) // CAP
    noise = jax.random.randint(jax.random.fold_in(key, 14), (block_count, slot_total), 0, 4096)
    boost = jnp.where(slot_home == hot_shard, 16384, 0)
    ranking_priority = (noise + shard_bias[slot_home][None, :] + boost[None, :]) * slot_total + jnp.arange(slot_total, dtype=jnp.int32)[None, :]
    chosen = lax.top_k(ranking_priority, pair_count)[1]
    home_shard = chosen // CAP
    shuffle_keys = jax.random.randint(jax.random.fold_in(key, 15), (block_count, pair_count), 0, 4096) * pair_count + jnp.arange(pair_count, dtype=jnp.int32)[None, :]
    order = jnp.argsort(shuffle_keys, axis=1)
    home_shard = jnp.take_along_axis(home_shard, order, axis=1)
    local_row = jax.random.randint(jax.random.fold_in(key, 16), (block_count, pair_count), 0, P_LOC)
    ids = inverse[home_shard * P_LOC + local_row]
    ids = ids.reshape(shard_count, cent_count, Q_DEV, CPD).transpose(0, 2, 1, 3).reshape(NQ, NCAND)
    return (home, ids.astype(jnp.int32))


def draw_passage_home(key, part):
    return index_tables(key)[0]


def draw_candidates(key, part):
    return index_tables(key)[1]


def draw_live_token_count(key, part):
    counts = jax.random.randint(jax.random.fold_in(key, 21), (NPASS,), 1, BLK + 1)
    spot = jax.random.randint(jax.random.fold_in(key, 22), (), 0, NPASS)
    return counts.at[spot].set(BLK).astype(jnp.int32)


def steps_of(own_key, extent, cuts, least, top_value):
    level = 1.0
    for axis_at, blocks in cuts:
        draws = jax.random.uniform(jax.random.fold_in(jax.random.fold_in(own_key, 6), axis_at), (blocks,), jnp.float32, least / len(cuts), top_value / len(cuts))
        level = level * jnp.repeat(jnp.exp(draws), extent[axis_at] // blocks).reshape((-1,) + (1,) * (len(extent) - 1 - axis_at))
    return level


def normal_values(rng, dims, spread, limit, pieces=(), kind=jnp.bfloat16):
    drawn = jax.random.normal(rng, dims, jnp.float32) * spread
    if len(pieces) > 0:
        drawn = steps_of(rng, dims, pieces, -0.22, 0.18) * drawn
    return jnp.clip(drawn, min=-limit, max=limit).astype(kind)


def setup_inputs(seed: int = 0) -> dict:
    key_of = jax.random.split(jax.random.key(seed), 7)
    return {
        "queries": normal_values(key_of[0], (NQ, QT, DIM), DIM ** -0.5, 0.5, ((0, 32),)),
        "centroids": normal_values(key_of[1], (CENT, DIM), DIM ** -0.5, 0.5, ((0, 8),)),
        "passage_tokens": normal_values(key_of[2], (NPASS, BLK, DIM), DIM ** -0.5, 0.5, ((0, 32),)),
        "live_token_count": draw_live_token_count(jax.random.fold_in(key_of[6], 71), 0),
        "passage_home": draw_passage_home(jax.random.fold_in(key_of[6], 71), 0),
        "candidates": draw_candidates(jax.random.fold_in(key_of[6], 71), 0),
    }


def reference(queries, centroids, passage_tokens, live_token_count, passage_home, candidates):
    query_rows = queries.reshape(NQ * QT, DIM)
    block_size = min(CENT, 4096)
    centroid_block_list = centroids.reshape(CENT // block_size, block_size, DIM)
    start_top = jnp.full((NQ * QT, NPROBE), -jnp.inf, jnp.float32)

    def advance(top_values, cent_block):
        scores = jnp.dot(query_rows, cent_block.T, preferred_element_type=jnp.float32)
        merged = lax.top_k(jnp.concatenate([top_values, scores], axis=1), NPROBE)[0]
        return merged, None

    top_values, _ = lax.scan(advance, start_top, centroid_block_list)
    probe_scores = top_values.reshape(NQ, QT, NPROBE)
    store_row = passage_home[candidates].astype(jnp.int32)

    def per_query(inputs):
        query, rows = inputs
        passage_row_matrix = passage_tokens[rows]
        lengths = live_token_count[rows]
        similarity_products = jnp.einsum("td,pjd->ptj", query.astype(jnp.float32), passage_row_matrix.astype(jnp.float32))
        in_length = jnp.arange(BLK, dtype=jnp.int32)[None, None, :] < lengths[:, None, None]
        similarity_products = jnp.where(in_length, similarity_products, -1e30)
        return jnp.sum(jnp.max(similarity_products, axis=2), axis=1)

    passage_scores = lax.map(per_query, (queries, store_row))
    return probe_scores, passage_scores
```

```python
import functools

import jax
import jax.numpy as jnp
from jax import lax
from jax.experimental import pallas as pl
from jax.experimental.pallas import tpu as pltpu
from jax.sharding import PartitionSpec as P

NPROBE = 4
LANES = 128
VMEM_LIMIT = 60 * 1024 * 1024
LEVELS = 3
GROUP = 16


def insert(running, x):
    out = []
    for rank, held in enumerate(running):
        out.append(jnp.maximum(held, x))
        if rank + 1 < len(running):
            x = jnp.minimum(held, x)
    return out


def streams(levels):
    return [2] * levels + [NPROBE]


def feed(xs, lists):
    for level in range(len(lists) - 1):
        half = len(xs) // 2
        losers = [jnp.minimum(a, b) for a, b in zip(xs[:half], xs[half:])]
        xs = [jnp.maximum(a, b) for a, b in zip(xs[:half], xs[half:])]
        for x in losers:
            lists[level] = insert(lists[level], x)
    for x in xs:
        lists[-1] = insert(lists[-1], x)


def merge_lists(a, b):
    m = [jnp.maximum(a[i], b[NPROBE - 1 - i]) for i in range(NPROBE)]
    for i, j in ((0, 2), (1, 3), (0, 1), (2, 3)):
        m[i], m[j] = jnp.maximum(m[i], m[j]), jnp.minimum(m[i], m[j])
    return m


def fold_sublanes(lists):
    for shift in (4, 2, 1):
        lists = merge_lists(lists, [pltpu.roll(t, shift, 0) for t in lists])
    return lists


def probe_kernel(q_ref, c_ref, o_ref, list_ref):
    step = pl.program_id(0)
    kept = streams(LEVELS)
    nq = q_ref.shape[0]

    @pl.when(step == 0)
    def _():
        list_ref[...] = jnp.full(list_ref.shape, -jnp.inf, jnp.float32)

    scores = lax.dot_general(
        c_ref[...], q_ref[...], (((1,), (1,)), ((), ())), preferred_element_type=jnp.float32
    )
    for col in range(0, nq, LANES):
        at = 0
        lists = []
        for k in kept:
            lists.append([list_ref[at + a, :, col : col + LANES] for a in range(k)])
            at += k
        for row in range(0, scores.shape[0], 8 * GROUP):
            feed([scores[row + 8 * r : row + 8 * r + 8, col : col + LANES] for r in range(GROUP)], lists)
        at = 0
        for held in lists:
            for a, t in enumerate(held):
                list_ref[at + a, :, col : col + LANES] = t
            at += len(held)

    @pl.when(step == pl.num_programs(0) - 1)
    def _():
        for tile in range(nq // LANES):
            at = 0
            lists = []
            for k in kept:
                lists.append([list_ref[at + a, :, tile * LANES : (tile + 1) * LANES] for a in range(k)])
                at += k
            top = lists[-1]
            for held in lists[:-1]:
                for x in held:
                    top = insert(top, x)
            top = fold_sublanes(top)
            for rank in range(NPROBE):
                row = rank * (nq // LANES) + tile
                o_ref[row : row + 1, :] = top[rank][0:1]


def probe(queries, centroids, block=4096):
    nq, dim = queries.shape
    total = centroids.shape[0]
    rows = NPROBE * nq // LANES
    return pl.pallas_call(
        probe_kernel,
        grid=(total // block,),
        in_specs=[pl.BlockSpec((nq, dim), lambda i: (0, 0)), pl.BlockSpec((block, dim), lambda i: (i, 0))],
        out_specs=pl.BlockSpec((rows, LANES), lambda i: (0, 0)),
        out_shape=jax.ShapeDtypeStruct((rows, LANES), jnp.float32),
        scratch_shapes=[pltpu.VMEM((sum(streams(LEVELS)), 8, nq), jnp.float32)],
        compiler_params=pltpu.CompilerParams(vmem_limit_bytes=VMEM_LIMIT),
        cost_estimate=pl.CostEstimate(
            flops=40 * nq * total * dim // 10, bytes_accessed=2 * total * dim, transcendentals=0
        ),
        name="probe",
    )(queries, centroids)


def prepare_kernel(count_ref, p_ref, home_ref, cand_ref, x_ref, shard_ref, local_ref):
    rows = lax.broadcasted_iota(jnp.int32, p_ref.shape[1:], 0)

    def one(p, carry):
        tokens = p_ref[p].astype(jnp.float32)
        x_ref[p] = jnp.where(rows < count_ref[p], tokens, tokens[0:1]).astype(x_ref.dtype)
        return carry

    lax.fori_loop(0, p_ref.shape[0], one, 0, unroll=2)
    nq, nk = cand_ref.shape
    cand = jnp.concatenate([cand_ref[...], jnp.zeros((nq, LANES - nk), jnp.int32)], axis=1)
    block, lane = cand // LANES, cand % LANES
    store = jnp.zeros((nq, LANES), jnp.int32)
    for b in range(home_ref.shape[0]):
        line = jnp.broadcast_to(home_ref[b : b + 1, :], (nq, LANES))
        store = jnp.where(block == b, jnp.take_along_axis(line, lane, axis=1), store)
    shard_ref[...] = store // p_ref.shape[0]
    local_ref[...] = store % p_ref.shape[0]


def prepare(counts, passages, home, candidates):
    nq = candidates.shape[0]
    index = jax.ShapeDtypeStruct((nq, LANES), jnp.int32)
    vmem = pl.BlockSpec(memory_space=pltpu.VMEM)
    return pl.pallas_call(
        prepare_kernel,
        in_specs=[pl.BlockSpec(memory_space=pltpu.SMEM), vmem, vmem, vmem],
        out_specs=[vmem, vmem, vmem],
        out_shape=[jax.ShapeDtypeStruct(passages.shape, passages.dtype), index, index],
        compiler_params=pltpu.CompilerParams(vmem_limit_bytes=VMEM_LIMIT),
        cost_estimate=pl.CostEstimate(flops=10**9, bytes_accessed=4 * passages.size, transcendentals=0),
        name="prepare",
    )(counts, passages, home.reshape(-1, LANES), candidates)


def maxsim_kernel(g_ref, x_ref, o_ref, best_ref, *, per, width, tokens):
    count, length, dim = x_ref.shape
    columns = g_ref.shape[0]

    def one(g, carry):
        at = pl.multiple_of(g * per, per)
        lhs = x_ref[pl.ds(at, per)].reshape(per * length, dim)
        for col in range(0, columns, width):
            dots = lax.dot_general(
                lhs, g_ref[col : col + width, :], (((1,), (1,)), ((), ())), preferred_element_type=jnp.float32
            )
            best = jnp.max(dots.reshape(per, length // 8, 8, width), axis=1)
            best_ref[pl.ds(at, per), col : col + width] = jnp.max(best, axis=1)
        return carry

    lax.fori_loop(0, count // per, one, 0)
    nq = o_ref.shape[0]
    owner = lax.broadcasted_iota(jnp.int32, (nq, columns), 1) // tokens
    pick = (owner == lax.broadcasted_iota(jnp.int32, (nq, columns), 0)).astype(jnp.bfloat16)
    rest = best_ref[...]
    total = jnp.zeros((nq, best_ref.shape[0]), jnp.float32)
    for _ in range(3):
        part = rest.astype(jnp.bfloat16)
        rest = rest - part.astype(jnp.float32)
        total += lax.dot_general(pick, part, (((1,), (1,)), ((), ())), preferred_element_type=jnp.float32)
    o_ref[...] = total


def maxsim(gathered, prepared, tokens):
    columns, dim = gathered.shape
    count, length, _ = prepared.shape
    nq = columns // tokens
    return pl.pallas_call(
        functools.partial(maxsim_kernel, per=16, width=512, tokens=tokens),
        out_shape=jax.ShapeDtypeStruct((nq, LANES), jnp.float32),
        scratch_shapes=[pltpu.VMEM((LANES, columns), jnp.float32)],
        compiler_params=pltpu.CompilerParams(vmem_limit_bytes=VMEM_LIMIT),
        cost_estimate=pl.CostEstimate(
            flops=2 * columns * count * length * dim, bytes_accessed=4 * prepared.size, transcendentals=0
        ),
        name="maxsim",
    )(gathered, prepared)


def finish_kernel(r_ref, shard_ref, local_ref, probe_ref, score_ref, *, shards, cents):
    lines = r_ref.shape[0] // cents
    half = shard_ref.shape[0] // 2
    nk = score_ref.shape[1]
    for j in range(2):
        home = shard_ref[pl.ds(j, half, stride=2), :]
        local = local_ref[pl.ds(j, half, stride=2), :]
        score = jnp.zeros(home.shape, jnp.float32)
        for s in range(shards):
            table = r_ref[pl.ds(2 * s + j, cents, stride=lines), :]
            score = jnp.where(home == s, jnp.take_along_axis(table, local, axis=1), score)
        score_ref[pl.ds(j, half, stride=2), :] = score[:, :nk]
    first = 2 * shards
    tiles = (lines - first) // NPROBE
    nt = probe_ref.shape[2]
    for tile in range(tiles):
        top = fold_sublanes(
            [r_ref[pl.ds(first + rank * tiles + tile, cents, stride=lines), :] for rank in range(NPROBE)]
        )
        four = jnp.concatenate([t[0:1] for t in top], axis=0)
        for i in range(LANES // nt):
            probe_ref[tile * (LANES // nt) + i] = four[:, i * nt : (i + 1) * nt]


def finish(received, shard_index, local_index, shards, cents, nq, nt, nk):
    return pl.pallas_call(
        functools.partial(finish_kernel, shards=shards, cents=cents),
        out_shape=[
            jax.ShapeDtypeStruct((nq, NPROBE, nt), jnp.float32),
            jax.ShapeDtypeStruct((nq, nk), jnp.float32),
        ],
        compiler_params=pltpu.CompilerParams(vmem_limit_bytes=VMEM_LIMIT),
        name="finish",
    )(received, shard_index, local_index)


def spread(block, copies):
    return jnp.broadcast_to(block[None], (copies,) + block.shape).reshape((-1,) + block.shape[1:])


def body(queries, centroids, passages, counts, home, candidates):
    nq, nt, dim = queries.shape
    nk = candidates.shape[1]
    shards, cents = lax.axis_size("shard"), lax.axis_size("cent")
    mine = nq // cents
    own = lax.dynamic_slice_in_dim(queries, lax.axis_index("cent") * mine, mine, 0).reshape(mine * nt, dim)
    gathered = lax.all_to_all(spread(own, shards), "shard", 0, 0, tiled=True)
    lists = probe(queries.reshape(nq * nt, dim), centroids)
    prepared, shard_index, local_index = prepare(counts, passages, home, candidates)
    table = maxsim(gathered, prepared, nt)
    returned = lax.all_to_all(table, "shard", 0, 0, tiled=True)
    final = spread(jnp.concatenate([returned, lists], axis=0), cents)
    received = lax.all_to_all(final, "cent", 0, 0, tiled=True)
    probe_scores, passage_scores = finish(received, shard_index, local_index, shards, cents, nq, nt, nk)
    return jnp.transpose(probe_scores, (0, 2, 1)), passage_scores


def solution(mesh):
    in_specs = (
        P("shard", None, None),
        P("cent", None),
        P("shard", None, None),
        P("shard"),
        P(),
        P("shard", "cent"),
    )
    out_specs = (P("shard", None, None), P("shard", "cent"))
    return jax.shard_map(body, mesh=mesh, in_specs=in_specs, out_specs=out_specs, check_vma=False)
```

```python
import functools

import jax
import jax.numpy as jnp
from jax import lax
from jax.experimental import pallas as pl
from jax.experimental.pallas import tpu as pltpu
from jax.sharding import PartitionSpec as P

NPROBE = 4
LANES = 128
MIB = 1024 * 1024
LEVELS = 3
GROUP = 16
ROWS = 16
PER = 16
FIRST = 5


def insert(running, x):
    out = []
    for rank, held in enumerate(running):
        out.append(jnp.maximum(held, x))
        if rank + 1 < len(running):
            x = jnp.minimum(held, x)
    return out


def streams(levels):
    return [2] * levels + [NPROBE]


def feed(xs, lists):
    for level in range(len(lists) - 1):
        half = len(xs) // 2
        losers = [jnp.minimum(a, b) for a, b in zip(xs[:half], xs[half:])]
        xs = [jnp.maximum(a, b) for a, b in zip(xs[:half], xs[half:])]
        for x in losers:
            lists[level] = insert(lists[level], x)
    for x in xs:
        lists[-1] = insert(lists[-1], x)


def merge_lists(a, b):
    m = [jnp.maximum(a[i], b[NPROBE - 1 - i]) for i in range(NPROBE)]
    for i, j in ((0, 2), (1, 3), (0, 1), (2, 3)):
        m[i], m[j] = jnp.maximum(m[i], m[j]), jnp.minimum(m[i], m[j])
    return m


def fold_sublanes(lists):
    for shift in (4, 2, 1):
        lists = merge_lists(lists, [pltpu.roll(t, shift, 0) for t in lists])
    return lists


def probe_kernel(q_ref, c_ref, before_ref, o_ref, list_ref):
    step = pl.program_id(0)
    kept = streams(LEVELS)
    nq = q_ref.shape[0]

    @pl.when(step == 0)
    def _():
        list_ref[...] = jnp.full(list_ref.shape, -jnp.inf, jnp.float32)

    scores = lax.dot_general(
        c_ref[...], q_ref[...], (((1,), (1,)), ((), ())), preferred_element_type=jnp.float32
    )
    for col in range(0, nq, LANES):
        at = 0
        lists = []
        for k in kept:
            lists.append([list_ref[at + a, :, col : col + LANES] for a in range(k)])
            at += k
        for row in range(0, scores.shape[0], 8 * GROUP):
            feed([scores[row + 8 * r : row + 8 * r + 8, col : col + LANES] for r in range(GROUP)], lists)
        at = 0
        for held in lists:
            for a, t in enumerate(held):
                list_ref[at + a, :, col : col + LANES] = t
            at += len(held)

    @pl.when(step == pl.num_programs(0) - 1)
    def _():
        for tile in range(nq // LANES):
            at = 0
            lists = []
            for k in kept:
                lists.append([list_ref[at + a, :, tile * LANES : (tile + 1) * LANES] for a in range(k)])
                at += k
            top = lists[-1]
            for held in lists[:-1]:
                for x in held:
                    top = insert(top, x)
            top = fold_sublanes(top)
            at_rows = [rank * (nq // LANES) + tile for rank in range(NPROBE)]
            top = merge_lists([t[0:1] for t in top], [before_ref[row : row + 1, :] for row in at_rows])
            for rank, row in enumerate(at_rows):
                o_ref[row : row + 1, :] = top[rank]


def probe(queries, centroids, before, first, steps, block=4096):
    nq, dim = queries.shape
    total = steps * block
    rows = NPROBE * nq // LANES
    return pl.pallas_call(
        probe_kernel,
        grid=(steps,),
        in_specs=[
            pl.BlockSpec((nq, dim), lambda i: (0, 0)),
            pl.BlockSpec((block, dim), lambda i: (first + i, 0)),
            pl.BlockSpec((rows, LANES), lambda i: (0, 0)),
        ],
        out_specs=pl.BlockSpec((rows, LANES), lambda i: (0, 0)),
        out_shape=jax.ShapeDtypeStruct((rows, LANES), jnp.float32),
        scratch_shapes=[pltpu.VMEM((sum(streams(LEVELS)), 8, nq), jnp.float32)],
        compiler_params=pltpu.CompilerParams(vmem_limit_bytes=60 * MIB),
        cost_estimate=pl.CostEstimate(
            flops=4 * nq * total * dim, bytes_accessed=2 * total * dim, transcendentals=0
        ),
        name=f"probe_{first}",
    )(queries, centroids, before)


def prepare_kernel(
    count_ref, p_ref, home_ref, cand_ref, x_ref, shard_ref, local_ref, place_ref, tiles_ref, next_ref, sorted_ref
):
    total, length, _ = p_ref.shape
    classes = length // ROWS
    rows = lax.broadcasted_iota(jnp.int32, p_ref.shape[1:], 0)
    lanes = lax.broadcasted_iota(jnp.int32, place_ref.shape, 1)

    def tiles_of(p):
        return (count_ref[p] + (ROWS - 1)) // ROWS

    for k in range(classes + 1):
        next_ref[k] = 0

    def tally(p, carry):
        k = classes - tiles_of(p) + 1
        next_ref[k] = next_ref[k] + 1
        return carry

    lax.fori_loop(0, total, tally, 0)
    for k in range(1, classes + 1):
        next_ref[k] = next_ref[k] + next_ref[k - 1]

    def one(p, places):
        tiles = tiles_of(p)
        at = next_ref[classes - tiles]
        next_ref[classes - tiles] = at + 1
        sorted_ref[at] = tiles
        tokens = p_ref[p].astype(jnp.float32)
        x_ref[at] = jnp.where(rows < count_ref[p], tokens, tokens[0:1]).astype(x_ref.dtype)
        return jnp.where(lanes == p, at, places)

    place_ref[...] = lax.fori_loop(0, total, one, jnp.zeros(place_ref.shape, jnp.int32))
    for g in range(total // PER):
        tiles_ref[g] = sorted_ref[g * PER]
    nq, nk = cand_ref.shape
    cand = jnp.concatenate([cand_ref[...], jnp.zeros((nq, LANES - nk), jnp.int32)], axis=1)
    block, lane = cand // LANES, cand % LANES
    store = jnp.zeros((nq, LANES), jnp.int32)
    for b in range(home_ref.shape[0]):
        line = jnp.broadcast_to(home_ref[b : b + 1, :], (nq, LANES))
        store = jnp.where(block == b, jnp.take_along_axis(line, lane, axis=1), store)
    shard_ref[...] = store // total
    local_ref[...] = store % total


def prepare(counts, passages, home, candidates):
    nq = candidates.shape[0]
    total, length, _ = passages.shape
    index = jax.ShapeDtypeStruct((nq, LANES), jnp.int32)
    vmem = pl.BlockSpec(memory_space=pltpu.VMEM)
    smem = pl.BlockSpec(memory_space=pltpu.SMEM)
    return pl.pallas_call(
        prepare_kernel,
        in_specs=[smem, vmem, vmem, vmem],
        out_specs=[vmem, vmem, vmem, vmem, smem],
        out_shape=[
            jax.ShapeDtypeStruct(passages.shape, passages.dtype),
            index,
            index,
            jax.ShapeDtypeStruct((8, LANES), jnp.int32),
            jax.ShapeDtypeStruct((total // PER,), jnp.int32),
        ],
        scratch_shapes=[pltpu.SMEM((length // ROWS + 1,), jnp.int32), pltpu.SMEM((total,), jnp.int32)],
        compiler_params=pltpu.CompilerParams(vmem_limit_bytes=60 * MIB),
        cost_estimate=pl.CostEstimate(flops=10**9, bytes_accessed=4 * passages.size, transcendentals=0),
        name="prepare",
    )(counts, passages, home.reshape(-1, LANES), candidates)


def maxsim_kernel(tiles_ref, g_ref, x_ref, place_ref, o_ref, best_ref, *, width, tokens):
    count, length, dim = x_ref.shape
    columns = g_ref.shape[0]
    best_ref[count:, :] = jnp.zeros((best_ref.shape[0] - count, columns), jnp.float32)

    def one(g, carry):
        at = pl.multiple_of(g * PER, PER)
        for tiles in range(1, length // ROWS + 1):
            rows = tiles * ROWS

            @pl.when(tiles_ref[g] == tiles)
            def _(rows=rows):
                lhs = x_ref[pl.ds(at, PER), :rows, :].reshape(PER * rows, dim)
                for col in range(0, columns, width):
                    dots = lax.dot_general(
                        lhs, g_ref[col : col + width, :], (((1,), (1,)), ((), ())), preferred_element_type=jnp.float32
                    )
                    best = jnp.max(dots.reshape(PER, rows // 8, 8, width), axis=1)
                    best_ref[pl.ds(at, PER), col : col + width] = jnp.max(best, axis=1)

        return carry

    lax.fori_loop(0, count // PER, one, 0)
    nq = o_ref.shape[0]
    owner = lax.broadcasted_iota(jnp.int32, (nq, columns), 1) // tokens
    pick = (owner == lax.broadcasted_iota(jnp.int32, (nq, columns), 0)).astype(jnp.bfloat16)
    rest = best_ref[...]
    total = jnp.zeros((nq, best_ref.shape[0]), jnp.float32)
    for _ in range(3):
        part = rest.astype(jnp.bfloat16)
        rest = rest - part.astype(jnp.float32)
        total += lax.dot_general(pick, part, (((1,), (1,)), ((), ())), preferred_element_type=jnp.float32)
    place = jnp.broadcast_to(place_ref[0:1, :], total.shape)
    o_ref[...] = jnp.take_along_axis(total, place, axis=1)


def maxsim(tiles, gathered, prepared, places, tokens):
    columns, dim = gathered.shape
    count, length, _ = prepared.shape
    nq = columns // tokens
    vmem = pl.BlockSpec(memory_space=pltpu.VMEM)
    return pl.pallas_call(
        functools.partial(maxsim_kernel, width=512, tokens=tokens),
        in_specs=[pl.BlockSpec(memory_space=pltpu.SMEM), vmem, vmem, vmem],
        out_specs=vmem,
        out_shape=jax.ShapeDtypeStruct((nq, LANES), jnp.float32),
        scratch_shapes=[pltpu.VMEM((LANES, columns), jnp.float32)],
        compiler_params=pltpu.CompilerParams(vmem_limit_bytes=24 * MIB),
        cost_estimate=pl.CostEstimate(
            flops=2 * columns * count * length * dim, bytes_accessed=4 * prepared.size, transcendentals=0
        ),
        name="maxsim",
    )(tiles, gathered, prepared, places)


def finish_kernel(r_ref, shard_ref, local_ref, probe_ref, score_ref, *, shards, cents):
    lines = r_ref.shape[0] // cents
    half = shard_ref.shape[0] // 2
    nk = score_ref.shape[1]
    for j in range(2):
        home = shard_ref[pl.ds(j, half, stride=2), :]
        local = local_ref[pl.ds(j, half, stride=2), :]
        score = jnp.zeros(home.shape, jnp.float32)
        for s in range(shards):
            table = r_ref[pl.ds(2 * s + j, cents, stride=lines), :]
            score = jnp.where(home == s, jnp.take_along_axis(table, local, axis=1), score)
        score_ref[pl.ds(j, half, stride=2), :] = score[:, :nk]
    first = 2 * shards
    tiles = (lines - first) // NPROBE
    nt = probe_ref.shape[2]
    for tile in range(tiles):
        top = fold_sublanes(
            [r_ref[pl.ds(first + rank * tiles + tile, cents, stride=lines), :] for rank in range(NPROBE)]
        )
        four = jnp.concatenate([t[0:1] for t in top], axis=0)
        for i in range(LANES // nt):
            probe_ref[tile * (LANES // nt) + i] = four[:, i * nt : (i + 1) * nt]


def finish(received, shard_index, local_index, shards, cents, nq, nt, nk):
    return pl.pallas_call(
        functools.partial(finish_kernel, shards=shards, cents=cents),
        out_shape=[
            jax.ShapeDtypeStruct((nq, NPROBE, nt), jnp.float32),
            jax.ShapeDtypeStruct((nq, nk), jnp.float32),
        ],
        compiler_params=pltpu.CompilerParams(vmem_limit_bytes=16 * MIB),
        name="finish",
    )(received, shard_index, local_index)


def spread(block, copies):
    return jnp.broadcast_to(block[None], (copies,) + block.shape).reshape((-1,) + block.shape[1:])


def body(queries, centroids, passages, counts, home, candidates):
    nq, nt, dim = queries.shape
    nk = candidates.shape[1]
    shards, cents = lax.axis_size("shard"), lax.axis_size("cent")
    mine = nq // cents
    own = lax.dynamic_slice_in_dim(queries, lax.axis_index("cent") * mine, mine, 0).reshape(mine * nt, dim)
    gathered = lax.all_to_all(spread(own, shards), "shard", 0, 0, tiled=True)
    tokens = queries.reshape(nq * nt, dim)
    blocks = centroids.shape[0] // 4096
    lists = probe(tokens, centroids, jnp.full((NPROBE * nq * nt // LANES, LANES), -jnp.inf, jnp.float32), 0, FIRST)
    prepared, shard_index, local_index, places, tiles = prepare(counts, passages, home, candidates)
    gathered, lists = lax.optimization_barrier((gathered, lists))
    table = maxsim(tiles, gathered, prepared, places, nt)
    table, lists = lax.optimization_barrier((table, lists))
    returned = lax.all_to_all(table, "shard", 0, 0, tiled=True)
    lists = probe(tokens, centroids, lists, FIRST, blocks - FIRST)
    final = spread(jnp.concatenate([returned, lists], axis=0), cents)
    received = lax.all_to_all(final, "cent", 0, 0, tiled=True)
    probe_scores, passage_scores = finish(received, shard_index, local_index, shards, cents, nq, nt, nk)
    return jnp.transpose(probe_scores, (0, 2, 1)), passage_scores


def solution(mesh):
    in_specs = (
        P("shard", None, None),
        P("cent", None),
        P("shard", None, None),
        P("shard"),
        P(),
        P("shard", "cent"),
    )
    out_specs = (P("shard", None, None), P("shard", "cent"))
    return jax.shard_map(body, mesh=mesh, in_specs=in_specs, out_specs=out_specs, check_vma=False)
```

```python
import functools

import jax
import jax.numpy as jnp
from jax import lax
from jax.experimental import pallas as pl
from jax.experimental.pallas import tpu as pltpu
from jax.sharding import PartitionSpec as P

NPROBE = 4
LANES = 128
MIB = 1024 * 1024
LEVELS = 3
GROUP = 16
ROWS = 16
CLASSES = 128 // ROWS
PER = 16
FIRST = 6


def insert(running, x):
    out = []
    for rank, held in enumerate(running):
        out.append(jnp.maximum(held, x))
        if rank + 1 < len(running):
            x = jnp.minimum(held, x)
    return out


def streams(levels):
    return [2] * levels + [NPROBE]


def feed(xs, lists):
    for level in range(len(lists) - 1):
        half = len(xs) // 2
        losers = [jnp.minimum(a, b) for a, b in zip(xs[:half], xs[half:])]
        xs = [jnp.maximum(a, b) for a, b in zip(xs[:half], xs[half:])]
        for x in losers:
            lists[level] = insert(lists[level], x)
    for x in xs:
        lists[-1] = insert(lists[-1], x)


def merge_lists(a, b):
    m = [jnp.maximum(a[i], b[NPROBE - 1 - i]) for i in range(NPROBE)]
    for i, j in ((0, 2), (1, 3), (0, 1), (2, 3)):
        m[i], m[j] = jnp.maximum(m[i], m[j]), jnp.minimum(m[i], m[j])
    return m


def fold_sublanes(lists):
    for shift in (4, 2, 1):
        lists = merge_lists(lists, [pltpu.roll(t, shift, 0) for t in lists])
    return lists


def probe_kernel(q_ref, c_ref, *refs):
    before_ref = refs[0] if len(refs) > 2 else None
    o_ref, list_ref = refs[-2:]
    step = pl.program_id(0)
    kept = streams(LEVELS)
    nq = q_ref.shape[0]

    @pl.when(step == 0)
    def _():
        list_ref[...] = jnp.full(list_ref.shape, -jnp.inf, jnp.float32)

    scores = lax.dot_general(
        c_ref[...], q_ref[...], (((1,), (1,)), ((), ())), preferred_element_type=jnp.float32
    )
    for col in range(0, nq, LANES):
        at = 0
        lists = []
        for k in kept:
            lists.append([list_ref[at + a, :, col : col + LANES] for a in range(k)])
            at += k
        for row in range(0, scores.shape[0], 8 * GROUP):
            feed([scores[row + 8 * r : row + 8 * r + 8, col : col + LANES] for r in range(GROUP)], lists)
        at = 0
        for held in lists:
            for a, t in enumerate(held):
                list_ref[at + a, :, col : col + LANES] = t
            at += len(held)

    @pl.when(step == pl.num_programs(0) - 1)
    def _():
        for tile in range(nq // LANES):
            at = 0
            lists = []
            for k in kept:
                lists.append([list_ref[at + a, :, tile * LANES : (tile + 1) * LANES] for a in range(k)])
                at += k
            top = lists[-1]
            for held in lists[:-1]:
                for x in held:
                    top = insert(top, x)
            top = fold_sublanes(top)
            at_rows = [rank * (nq // LANES) + tile for rank in range(NPROBE)]
            top = [t[0:1] for t in top]
            if before_ref is not None:
                top = merge_lists(top, [before_ref[row : row + 1, :] for row in at_rows])
            for rank, row in enumerate(at_rows):
                o_ref[row : row + 1, :] = top[rank]


def probe(queries, centroids, before, first, steps, block=4096):
    nq, dim = queries.shape
    total = steps * block
    rows = NPROBE * nq // LANES
    return pl.pallas_call(
        probe_kernel,
        grid=(steps,),
        in_specs=[
            pl.BlockSpec((nq, dim), lambda i: (0, 0)),
            pl.BlockSpec((block, dim), lambda i: (first + i, 0)),
        ]
        + [pl.BlockSpec((rows, LANES), lambda i: (0, 0))] * len(before),
        out_specs=pl.BlockSpec((rows, LANES), lambda i: (0, 0)),
        out_shape=jax.ShapeDtypeStruct((rows, LANES), jnp.float32),
        scratch_shapes=[pltpu.VMEM((sum(streams(LEVELS)), 8, nq), jnp.float32)],
        compiler_params=pltpu.CompilerParams(vmem_limit_bytes=58 * MIB),
        cost_estimate=pl.CostEstimate(
            flops=4 * nq * total * dim, bytes_accessed=2 * total * dim, transcendentals=0
        ),
        name=f"probe_{first}",
    )(queries, centroids, *before)


def prepare_kernel(count_ref, home_ref, cand_ref, shard_ref, local_ref, place_ref, order_ref, tiles_ref, next_ref):
    total = order_ref.shape[0]
    lanes = lax.broadcasted_iota(jnp.int32, place_ref.shape, 1)

    def tiles_of(p):
        return lax.shift_right_logical(count_ref[p] + (ROWS - 1), ROWS.bit_length() - 1)

    for k in range(CLASSES + 1):
        next_ref[k] = 0

    def tally(p, carry):
        k = CLASSES + 1 - tiles_of(p)
        next_ref[k] = next_ref[k] + 1
        return carry

    lax.fori_loop(0, total, tally, 0, unroll=8)
    for k in range(1, CLASSES + 1):
        next_ref[k] = next_ref[k] + next_ref[k - 1]

    def one(p, places):
        k = CLASSES - tiles_of(p)
        at = next_ref[k]
        next_ref[k] = at + 1
        order_ref[at] = p
        return jnp.where(lanes == p, at, places)

    place_ref[...] = lax.fori_loop(0, total, one, jnp.zeros(place_ref.shape, jnp.int32), unroll=8)
    for g in range(total // PER):
        tiles_ref[g] = tiles_of(order_ref[g * PER])
    nq, nk = cand_ref.shape
    cand = jnp.concatenate([cand_ref[...], jnp.zeros((nq, LANES - nk), jnp.int32)], axis=1)
    block, lane = lax.shift_right_logical(cand, 7), jnp.bitwise_and(cand, LANES - 1)
    store = jnp.zeros((nq, LANES), jnp.int32)
    for b in range(home_ref.shape[0]):
        line = jnp.broadcast_to(home_ref[b : b + 1, :], (nq, LANES))
        store = jnp.where(block == b, jnp.take_along_axis(line, lane, axis=1), store)
    shard_ref[...] = store // total
    local_ref[...] = store % total


def prepare(counts, home, candidates):
    nq = candidates.shape[0]
    total = counts.shape[0]
    index = jax.ShapeDtypeStruct((nq, LANES), jnp.int32)
    vmem = pl.BlockSpec(memory_space=pltpu.VMEM)
    smem = pl.BlockSpec(memory_space=pltpu.SMEM)
    return pl.pallas_call(
        prepare_kernel,
        in_specs=[smem, vmem, vmem],
        out_specs=[vmem, vmem, vmem, smem, smem],
        out_shape=[
            index,
            index,
            jax.ShapeDtypeStruct((8, LANES), jnp.int32),
            jax.ShapeDtypeStruct((total,), jnp.int32),
            jax.ShapeDtypeStruct((total // PER,), jnp.int32),
        ],
        scratch_shapes=[pltpu.SMEM((CLASSES + 1,), jnp.int32)],
        compiler_params=pltpu.CompilerParams(vmem_limit_bytes=58 * MIB),
        cost_estimate=pl.CostEstimate(flops=10**9, bytes_accessed=10**5, transcendentals=0),
        name="prepare",
    )(counts, home.reshape(-1, LANES), candidates)


def maxsim_kernel(count_ref, order_ref, tiles_ref, g_ref, p_ref, place_ref, o_ref, best_ref, lhs_ref, *, width, tokens):
    count, length, dim = p_ref.shape
    columns = g_ref.shape[0]
    best_ref[count:, :] = jnp.zeros((best_ref.shape[0] - count, columns), jnp.float32)

    def one(g, carry):
        at = pl.multiple_of(g * PER, PER)
        for tiles in range(1, length // ROWS + 1):
            rows = tiles * ROWS

            @pl.when(tiles_ref[g] == tiles)
            def _(rows=rows):
                index = lax.broadcasted_iota(jnp.int32, (rows, dim), 0)
                for i in range(PER):
                    p = order_ref[at + i]
                    block = p_ref[p, :rows, :].astype(jnp.float32)
                    block = jnp.where(index < count_ref[p], block, block[0:1])
                    lhs_ref[i * rows : (i + 1) * rows, :] = block.astype(lhs_ref.dtype)
                lhs = lhs_ref[: PER * rows, :]
                for col in range(0, columns, width):
                    dots = lax.dot_general(
                        lhs, g_ref[col : col + width, :], (((1,), (1,)), ((), ())), preferred_element_type=jnp.float32
                    )
                    best = jnp.max(dots.reshape(PER, rows // 8, 8, width), axis=1)
                    best_ref[pl.ds(at, PER), col : col + width] = jnp.max(best, axis=1)

        return carry

    lax.fori_loop(0, count // PER, one, 0)
    nq = o_ref.shape[0]
    owner = lax.broadcasted_iota(jnp.int32, (nq, columns), 1) // tokens
    pick = (owner == lax.broadcasted_iota(jnp.int32, (nq, columns), 0)).astype(jnp.bfloat16)
    rest = best_ref[...]
    total = jnp.zeros((nq, best_ref.shape[0]), jnp.float32)
    for _ in range(3):
        part = rest.astype(jnp.bfloat16)
        rest = rest - part.astype(jnp.float32)
        total += lax.dot_general(pick, part, (((1,), (1,)), ((), ())), preferred_element_type=jnp.float32)
    place = jnp.broadcast_to(place_ref[0:1, :], total.shape)
    o_ref[...] = jnp.take_along_axis(total, place, axis=1)


def maxsim(counts, order, tiles, gathered, passages, places, tokens, width=512):
    columns, dim = gathered.shape
    count, length, _ = passages.shape
    nq = columns // tokens
    vmem = pl.BlockSpec(memory_space=pltpu.VMEM)
    smem = pl.BlockSpec(memory_space=pltpu.SMEM)
    return pl.pallas_call(
        functools.partial(maxsim_kernel, width=width, tokens=tokens),
        in_specs=[smem, smem, smem, vmem, vmem, vmem],
        out_specs=vmem,
        out_shape=jax.ShapeDtypeStruct((nq, LANES), jnp.float32),
        scratch_shapes=[pltpu.VMEM((LANES, columns), jnp.float32), pltpu.VMEM((PER * length, dim), jnp.bfloat16)],
        compiler_params=pltpu.CompilerParams(vmem_limit_bytes=40 * MIB),
        cost_estimate=pl.CostEstimate(
            flops=2 * columns * count * length * dim, bytes_accessed=2 * passages.size, transcendentals=0
        ),
        name="maxsim",
    )(counts, order, tiles, gathered, passages, places)


def finish_kernel(r_ref, shard_ref, local_ref, probe_ref, score_ref, *, shards, cents):
    lines = r_ref.shape[0] // cents
    half = shard_ref.shape[0] // 2
    nk = score_ref.shape[1]
    for j in range(2):
        home = shard_ref[pl.ds(j, half, stride=2), :]
        local = local_ref[pl.ds(j, half, stride=2), :]
        score = jnp.zeros(home.shape, jnp.float32)
        for s in range(shards):
            table = r_ref[pl.ds(2 * s + j, cents, stride=lines), :]
            score = jnp.where(home == s, jnp.take_along_axis(table, local, axis=1), score)
        score_ref[pl.ds(j, half, stride=2), :] = score[:, :nk]
    first = 2 * shards
    tiles = (lines - first) // NPROBE
    nt = probe_ref.shape[2]
    for tile in range(tiles):
        top = fold_sublanes(
            [r_ref[pl.ds(first + rank * tiles + tile, cents, stride=lines), :] for rank in range(NPROBE)]
        )
        four = jnp.concatenate([t[0:1] for t in top], axis=0)
        for i in range(LANES // nt):
            probe_ref[tile * (LANES // nt) + i] = four[:, i * nt : (i + 1) * nt]


def finish(received, shard_index, local_index, shards, cents, nq, nt, nk):
    return pl.pallas_call(
        functools.partial(finish_kernel, shards=shards, cents=cents),
        out_shape=[
            jax.ShapeDtypeStruct((nq, NPROBE, nt), jnp.float32),
            jax.ShapeDtypeStruct((nq, nk), jnp.float32),
        ],
        compiler_params=pltpu.CompilerParams(vmem_limit_bytes=16 * MIB),
        name="finish",
    )(received, shard_index, local_index)


def copies_kernel(at_ref, x_ref, o_ref):
    rows = o_ref.shape[1]
    block = x_ref[pl.ds(pl.multiple_of(at_ref[0] * rows, rows), rows), :]
    for k in range(o_ref.shape[0]):
        o_ref[k] = block


def copies_of_part(x, at, rows, copies):
    vmem = pl.BlockSpec(memory_space=pltpu.VMEM)
    return pl.pallas_call(
        copies_kernel,
        in_specs=[pl.BlockSpec(memory_space=pltpu.SMEM), vmem],
        out_specs=vmem,
        out_shape=jax.ShapeDtypeStruct((copies, rows, x.shape[1]), x.dtype),
        name="copies",
    )(jnp.full((1,), at, jnp.int32), x)


def joined_kernel(a_ref, b_ref, o_ref):
    for k in range(o_ref.shape[0]):
        o_ref[k, : a_ref.shape[0]] = a_ref[...]
        o_ref[k, a_ref.shape[0] :] = b_ref[...]


def copies_of_both(a, b, copies):
    return pl.pallas_call(
        joined_kernel,
        out_shape=jax.ShapeDtypeStruct((copies, a.shape[0] + b.shape[0], a.shape[1]), a.dtype),
        name="joined",
    )(a, b)


def body(queries, centroids, passages, counts, home, candidates):
    nq, nt, dim = queries.shape
    nk = candidates.shape[1]
    shards, cents = lax.axis_size("shard"), lax.axis_size("cent")
    mine = nq // cents
    tokens = queries.reshape(nq * nt, dim)
    own = copies_of_part(tokens, lax.axis_index("cent"), mine * nt, shards)
    gathered = lax.all_to_all(own.reshape(-1, dim), "shard", 0, 0, tiled=True)
    blocks = centroids.shape[0] // 4096
    lists = probe(tokens, centroids, (), 0, FIRST)
    shard_index, local_index, places, order, tiles = prepare(counts, home, candidates)
    gathered, lists = lax.optimization_barrier((gathered, lists))
    table = maxsim(counts, order, tiles, gathered, passages, places, nt)
    table, lists = lax.optimization_barrier((table, lists))
    returned = lax.all_to_all(table, "shard", 0, 0, tiled=True)
    lists = probe(tokens, centroids, (lists,), FIRST, blocks - FIRST)
    final = copies_of_both(returned, lists, cents)
    received = lax.all_to_all(final.reshape(-1, LANES), "cent", 0, 0, tiled=True)
    probe_scores, passage_scores = finish(received, shard_index, local_index, shards, cents, nq, nt, nk)
    return jnp.transpose(probe_scores, (0, 2, 1)), passage_scores


def solution(mesh):
    in_specs = (
        P("shard", None, None),
        P("cent", None),
        P("shard", None, None),
        P("shard"),
        P(),
        P("shard", "cent"),
    )
    out_specs = (P("shard", None, None), P("shard", "cent"))
    return jax.shard_map(body, mesh=mesh, in_specs=in_specs, out_specs=out_specs, check_vma=False)
```

```python
import functools

import jax
import jax.numpy as jnp
from jax import lax
from jax.experimental import pallas as pl
from jax.experimental.pallas import tpu as pltpu
from jax.sharding import PartitionSpec as P

NPROBE = 4
LANES = 128
MIB = 1024 * 1024
LEVELS = 3
GROUP = 16
ROWS = 16
CLASSES = 128 // ROWS
PER = 16
FIRST = 7


def insert(running, x):
    out = []
    for rank, held in enumerate(running):
        out.append(jnp.maximum(held, x))
        if rank + 1 < len(running):
            x = jnp.minimum(held, x)
    return out


def streams(levels):
    return [2] * levels + [NPROBE]


def feed(xs, lists):
    for level in range(len(lists) - 1):
        half = len(xs) // 2
        losers = [jnp.minimum(a, b) for a, b in zip(xs[:half], xs[half:])]
        xs = [jnp.maximum(a, b) for a, b in zip(xs[:half], xs[half:])]
        for x in losers:
            lists[level] = insert(lists[level], x)
    for x in xs:
        lists[-1] = insert(lists[-1], x)


def merge_lists(a, b):
    m = [jnp.maximum(a[i], b[NPROBE - 1 - i]) for i in range(NPROBE)]
    for i, j in ((0, 2), (1, 3), (0, 1), (2, 3)):
        m[i], m[j] = jnp.maximum(m[i], m[j]), jnp.minimum(m[i], m[j])
    return m


def fold_sublanes(lists):
    for shift in (4, 2, 1):
        lists = merge_lists(lists, [pltpu.roll(t, shift, 0) for t in lists])
    return lists


def probe_kernel(q_ref, c_ref, *refs):
    before_ref = refs[0] if len(refs) > 2 else None
    o_ref, list_ref = refs[-2:]
    step = pl.program_id(0)
    kept = streams(LEVELS)
    nq = q_ref.shape[0]

    @pl.when(step == 0)
    def _():
        list_ref[...] = jnp.full(list_ref.shape, -jnp.inf, jnp.float32)

    scores = lax.dot_general(
        c_ref[...], q_ref[...], (((1,), (1,)), ((), ())), preferred_element_type=jnp.float32
    )
    for col in range(0, nq, LANES):
        at = 0
        lists = []
        for k in kept:
            lists.append([list_ref[at + a, :, col : col + LANES] for a in range(k)])
            at += k
        for row in range(0, scores.shape[0], 8 * GROUP):
            feed([scores[row + 8 * r : row + 8 * r + 8, col : col + LANES] for r in range(GROUP)], lists)
        at = 0
        for held in lists:
            for a, t in enumerate(held):
                list_ref[at + a, :, col : col + LANES] = t
            at += len(held)

    @pl.when(step == pl.num_programs(0) - 1)
    def _():
        for tile in range(nq // LANES):
            at = 0
            lists = []
            for k in kept:
                lists.append([list_ref[at + a, :, tile * LANES : (tile + 1) * LANES] for a in range(k)])
                at += k
            top = lists[-1]
            for held in lists[:-1]:
                for x in held:
                    top = insert(top, x)
            top = fold_sublanes(top)
            at_rows = [rank * (nq // LANES) + tile for rank in range(NPROBE)]
            top = [t[0:1] for t in top]
            if before_ref is not None:
                top = merge_lists(top, [before_ref[row : row + 1, :] for row in at_rows])
            for rank, row in enumerate(at_rows):
                o_ref[row : row + 1, :] = top[rank]


def probe(queries, centroids, before, first, steps, block=4096):
    nq, dim = queries.shape
    total = steps * block
    rows = NPROBE * nq // LANES
    return pl.pallas_call(
        probe_kernel,
        grid=(steps,),
        in_specs=[
            pl.BlockSpec((nq, dim), lambda i: (0, 0)),
            pl.BlockSpec((block, dim), lambda i: (first + i, 0)),
        ]
        + [pl.BlockSpec((rows, LANES), lambda i: (0, 0))] * len(before),
        out_specs=pl.BlockSpec((rows, LANES), lambda i: (0, 0)),
        out_shape=jax.ShapeDtypeStruct((rows, LANES), jnp.float32),
        scratch_shapes=[pltpu.VMEM((sum(streams(LEVELS)), 8, nq), jnp.float32)],
        compiler_params=pltpu.CompilerParams(vmem_limit_bytes=24 * MIB),
        cost_estimate=pl.CostEstimate(
            flops=4 * nq * total * dim, bytes_accessed=2 * total * dim, transcendentals=0
        ),
        name=f"probe_{first}",
    )(queries, centroids, *before)


def prepare_kernel(count_ref, home_ref, cand_ref, shard_ref, local_ref, place_ref, order_ref, tiles_ref, next_ref):
    total = order_ref.shape[0]
    lanes = lax.broadcasted_iota(jnp.int32, place_ref.shape, 1)

    def tiles_of(p):
        return lax.shift_right_logical(count_ref[p] + (ROWS - 1), ROWS.bit_length() - 1)

    for k in range(CLASSES + 1):
        next_ref[k] = 0

    def tally(p, carry):
        k = CLASSES + 1 - tiles_of(p)
        next_ref[k] = next_ref[k] + 1
        return carry

    lax.fori_loop(0, total, tally, 0, unroll=8)
    for k in range(1, CLASSES + 1):
        next_ref[k] = next_ref[k] + next_ref[k - 1]

    def one(p, places):
        k = CLASSES - tiles_of(p)
        at = next_ref[k]
        next_ref[k] = at + 1
        order_ref[at] = p
        return jnp.where(lanes == p, at, places)

    place_ref[...] = lax.fori_loop(0, total, one, jnp.zeros(place_ref.shape, jnp.int32), unroll=8)
    for g in range(total // PER):
        tiles_ref[g] = tiles_of(order_ref[g * PER])
    nq, nk = cand_ref.shape
    cand = jnp.concatenate([cand_ref[...], jnp.zeros((nq, LANES - nk), jnp.int32)], axis=1)
    block, lane = lax.shift_right_logical(cand, 7), jnp.bitwise_and(cand, LANES - 1)
    store = jnp.zeros((nq, LANES), jnp.int32)
    for b in range(home_ref.shape[0]):
        line = jnp.broadcast_to(home_ref[b : b + 1, :], (nq, LANES))
        store = jnp.where(block == b, jnp.take_along_axis(line, lane, axis=1), store)
    shard_ref[...] = store // total
    local_ref[...] = store % total


def prepare(counts, home, candidates):
    nq = candidates.shape[0]
    total = counts.shape[0]
    index = jax.ShapeDtypeStruct((nq, LANES), jnp.int32)
    vmem = pl.BlockSpec(memory_space=pltpu.VMEM)
    smem = pl.BlockSpec(memory_space=pltpu.SMEM)
    return pl.pallas_call(
        prepare_kernel,
        in_specs=[smem, vmem, vmem],
        out_specs=[vmem, vmem, vmem, smem, smem],
        out_shape=[
            index,
            index,
            jax.ShapeDtypeStruct((8, LANES), jnp.int32),
            jax.ShapeDtypeStruct((total,), jnp.int32),
            jax.ShapeDtypeStruct((total // PER,), jnp.int32),
        ],
        scratch_shapes=[pltpu.SMEM((CLASSES + 1,), jnp.int32)],
        compiler_params=pltpu.CompilerParams(vmem_limit_bytes=58 * MIB),
        cost_estimate=pl.CostEstimate(flops=10**9, bytes_accessed=10**5, transcendentals=0),
        name="prepare",
    )(counts, home.reshape(-1, LANES), candidates)


def maxsim_kernel(count_ref, order_ref, tiles_ref, g_ref, p_ref, place_ref, o_ref, best_ref, lhs_ref, *, width, tokens):
    count, length, dim = p_ref.shape
    columns = g_ref.shape[0]
    best_ref[count:, :] = jnp.zeros((best_ref.shape[0] - count, columns), jnp.float32)

    def one(g, carry):
        at = pl.multiple_of(g * PER, PER)
        for tiles in range(1, length // ROWS + 1):
            rows = tiles * ROWS

            @pl.when(tiles_ref[g] == tiles)
            def _(rows=rows):
                index = lax.broadcasted_iota(jnp.int32, (rows, dim), 0)
                for i in range(PER):
                    p = order_ref[at + i]
                    block = p_ref[p, :rows, :].astype(jnp.float32)
                    block = jnp.where(index < count_ref[p], block, block[0:1])
                    lhs_ref[i * rows : (i + 1) * rows, :] = block.astype(lhs_ref.dtype)
                lhs = lhs_ref[: PER * rows, :]
                for col in range(0, columns, width):
                    dots = lax.dot_general(
                        lhs, g_ref[col : col + width, :], (((1,), (1,)), ((), ())), preferred_element_type=jnp.float32
                    )
                    best = jnp.max(dots.reshape(PER, rows // 8, 8, width), axis=1)
                    best_ref[pl.ds(at, PER), col : col + width] = jnp.max(best, axis=1)

        return carry

    lax.fori_loop(0, count // PER, one, 0)
    nq = o_ref.shape[0]
    owner = lax.broadcasted_iota(jnp.int32, (nq, columns), 1) // tokens
    pick = (owner == lax.broadcasted_iota(jnp.int32, (nq, columns), 0)).astype(jnp.bfloat16)
    rest = best_ref[...]
    total = jnp.zeros((nq, best_ref.shape[0]), jnp.float32)
    for _ in range(3):
        part = rest.astype(jnp.bfloat16)
        rest = rest - part.astype(jnp.float32)
        total += lax.dot_general(pick, part, (((1,), (1,)), ((), ())), preferred_element_type=jnp.float32)
    place = jnp.broadcast_to(place_ref[0:1, :], total.shape)
    o_ref[...] = jnp.take_along_axis(total, place, axis=1)


def maxsim(counts, order, tiles, gathered, passages, places, tokens, width=512):
    columns, dim = gathered.shape
    count, length, _ = passages.shape
    nq = columns // tokens
    vmem = pl.BlockSpec(memory_space=pltpu.VMEM)
    smem = pl.BlockSpec(memory_space=pltpu.SMEM)
    return pl.pallas_call(
        functools.partial(maxsim_kernel, width=width, tokens=tokens),
        in_specs=[smem, smem, smem, vmem, vmem, vmem],
        out_specs=vmem,
        out_shape=jax.ShapeDtypeStruct((nq, LANES), jnp.float32),
        scratch_shapes=[pltpu.VMEM((LANES, columns), jnp.float32), pltpu.VMEM((PER * length, dim), jnp.bfloat16)],
        compiler_params=pltpu.CompilerParams(vmem_limit_bytes=40 * MIB),
        cost_estimate=pl.CostEstimate(
            flops=2 * columns * count * length * dim, bytes_accessed=2 * passages.size, transcendentals=0
        ),
        name="maxsim",
    )(counts, order, tiles, gathered, passages, places)


def finish_kernel(r_ref, shard_ref, local_ref, probe_ref, score_ref, *, shards, cents):
    lines = r_ref.shape[0] // cents
    half = shard_ref.shape[0] // 2
    nk = score_ref.shape[1]
    for j in range(2):
        home = shard_ref[pl.ds(j, half, stride=2), :]
        local = local_ref[pl.ds(j, half, stride=2), :]
        score = jnp.zeros(home.shape, jnp.float32)
        for s in range(shards):
            table = r_ref[pl.ds(2 * s + j, cents, stride=lines), :]
            score = jnp.where(home == s, jnp.take_along_axis(table, local, axis=1), score)
        score_ref[pl.ds(j, half, stride=2), :] = score[:, :nk]
    first = 2 * shards
    tiles = (lines - first) // NPROBE
    nt = probe_ref.shape[2]
    for tile in range(tiles):
        top = fold_sublanes(
            [r_ref[pl.ds(first + rank * tiles + tile, cents, stride=lines), :] for rank in range(NPROBE)]
        )
        four = jnp.concatenate([t[0:1] for t in top], axis=0)
        for i in range(LANES // nt):
            probe_ref[tile * (LANES // nt) + i] = four[:, i * nt : (i + 1) * nt]


def finish(received, shard_index, local_index, shards, cents, nq, nt, nk):
    return pl.pallas_call(
        functools.partial(finish_kernel, shards=shards, cents=cents),
        out_shape=[
            jax.ShapeDtypeStruct((nq, NPROBE, nt), jnp.float32),
            jax.ShapeDtypeStruct((nq, nk), jnp.float32),
        ],
        compiler_params=pltpu.CompilerParams(vmem_limit_bytes=16 * MIB),
        name="finish",
    )(received, shard_index, local_index)


def spread(block, copies):
    return jnp.broadcast_to(block[None], (copies,) + block.shape).reshape((-1,) + block.shape[1:])


def body(queries, centroids, passages, counts, home, candidates):
    nq, nt, dim = queries.shape
    nk = candidates.shape[1]
    shards, cents = lax.axis_size("shard"), lax.axis_size("cent")
    mine = nq // cents
    tokens = queries.reshape(nq * nt, dim)
    own = lax.dynamic_slice_in_dim(tokens, lax.axis_index("cent") * mine * nt, mine * nt, 0)
    gathered = lax.all_to_all(spread(own, shards), "shard", 0, 0, tiled=True)
    blocks = centroids.shape[0] // 4096
    centroids = pltpu.with_memory_space_constraint(centroids, pltpu.HBM)
    lists = probe(tokens, centroids, (), 0, FIRST)
    shard_index, local_index, places, order, tiles = prepare(counts, home, candidates)
    gathered, lists = lax.optimization_barrier((gathered, lists))
    table = maxsim(counts, order, tiles, gathered, passages, places, nt)
    table, lists = lax.optimization_barrier((table, lists))
    returned = lax.all_to_all(table, "shard", 0, 0, tiled=True)
    lists = probe(tokens, centroids, (lists,), FIRST, blocks - FIRST)
    final = spread(jnp.concatenate([returned, lists], axis=0), cents)
    received = lax.all_to_all(final, "cent", 0, 0, tiled=True)
    probe_scores, passage_scores = finish(received, shard_index, local_index, shards, cents, nq, nt, nk)
    return jnp.transpose(probe_scores, (0, 2, 1)), passage_scores


def solution(mesh):
    in_specs = (
        P("shard", None, None),
        P("cent", None),
        P("shard", None, None),
        P("shard"),
        P(),
        P("shard", "cent"),
    )
    out_specs = (P("shard", None, None), P("shard", "cent"))
    return jax.shard_map(body, mesh=mesh, in_specs=in_specs, out_specs=out_specs, check_vma=False)
```

```python
import functools

import jax
import jax.numpy as jnp
from jax import lax
from jax.experimental import pallas as pl
from jax.experimental.pallas import tpu as pltpu
from jax.sharding import PartitionSpec as P

NPROBE = 4
LANES = 128
MIB = 1024 * 1024
LEVELS = 3
GROUP = 16
ROWS = 16
PER = 16
SENT = 256


def insert(running, x):
    out = []
    for rank, held in enumerate(running):
        out.append(jnp.maximum(held, x))
        if rank + 1 < len(running):
            x = jnp.minimum(held, x)
    return out


def streams(levels):
    return [2] * levels + [NPROBE]


def feed(xs, lists):
    for level in range(len(lists) - 1):
        half = len(xs) // 2
        losers = [jnp.minimum(a, b) for a, b in zip(xs[:half], xs[half:])]
        xs = [jnp.maximum(a, b) for a, b in zip(xs[:half], xs[half:])]
        for x in losers:
            lists[level] = insert(lists[level], x)
    for x in xs:
        lists[-1] = insert(lists[-1], x)


def merge_lists(a, b):
    m = [jnp.maximum(a[i], b[NPROBE - 1 - i]) for i in range(NPROBE)]
    for i, j in ((0, 2), (1, 3), (0, 1), (2, 3)):
        m[i], m[j] = jnp.maximum(m[i], m[j]), jnp.minimum(m[i], m[j])
    return m


def fold_sublanes(lists):
    for shift in (4, 2, 1):
        lists = merge_lists(lists, [pltpu.roll(t, shift, 0) for t in lists])
    return lists


def probe_kernel(q_ref, c_ref, o_ref, list_ref):
    step = pl.program_id(0)
    kept = streams(LEVELS)
    nq = q_ref.shape[0]

    def held_lists(col):
        at, lists = 0, []
        for k in kept:
            lists.append([list_ref[at + a, :, col : col + LANES] for a in range(k)])
            at += k
        return lists

    @pl.when(step == 0)
    def _():
        list_ref[...] = jnp.full(list_ref.shape, -jnp.inf, jnp.float32)
        o_ref[...] = jnp.zeros(o_ref.shape, jnp.float32)

    scores = lax.dot_general(
        c_ref[...], q_ref[...], (((1,), (1,)), ((), ())), preferred_element_type=jnp.float32
    )
    for col in range(0, nq, LANES):
        lists = held_lists(col)
        for row in range(0, scores.shape[0], 8 * GROUP):
            feed([scores[row + 8 * r : row + 8 * r + 8, col : col + LANES] for r in range(GROUP)], lists)
        for at, t in enumerate(sum(lists, [])):
            list_ref[at, :, col : col + LANES] = t

    @pl.when(step == pl.num_programs(0) - 1)
    def _():
        for tile in range(nq // LANES):
            lists = held_lists(tile * LANES)
            top = lists[-1]
            for x in sum(lists[:-1], []):
                top = insert(top, x)
            top = fold_sublanes(top)
            for rank in range(NPROBE):
                row = rank * (nq // LANES) + tile
                o_ref[row : row + 1, :] = top[rank][0:1]


def probe(queries, centroids, rows, block=4096):
    nq, dim = queries.shape
    total = centroids.shape[0]
    return pl.pallas_call(
        probe_kernel,
        grid=(total // block,),
        in_specs=[pl.BlockSpec((nq, dim), lambda i: (0, 0)), pl.BlockSpec((block, dim), lambda i: (i, 0))],
        out_specs=pl.BlockSpec((rows, LANES), lambda i: (0, 0)),
        out_shape=jax.ShapeDtypeStruct((rows, LANES), jnp.float32),
        scratch_shapes=[pltpu.VMEM((sum(streams(LEVELS)), 8, nq), jnp.float32)],
        compiler_params=pltpu.CompilerParams(vmem_limit_bytes=58 * MIB),
        cost_estimate=pl.CostEstimate(
            flops=4 * nq * total * dim, bytes_accessed=2 * total * dim, transcendentals=0
        ),
        name="probe",
    )(queries, centroids)


def prepare_kernel(count_ref, home_ref, cand_ref, shard_ref, local_ref, place_ref, order_ref, tiles_ref):
    total = count_ref.shape[1]
    counts = jnp.concatenate([count_ref[...], jnp.full((1, LANES - total), 1 - ROWS, jnp.int32)], axis=1)
    tiles = lax.shift_right_arithmetic(counts + (ROWS - 1), ROWS.bit_length() - 1)
    lane = lax.broadcasted_iota(jnp.int32, (LANES, LANES), 1).astype(jnp.float32)
    tiles_across = jnp.broadcast_to(tiles.astype(jnp.float32), (LANES, LANES))
    across = tiles_across * LANES - lane
    down = across.T
    place_across = jnp.sum(jnp.where(down > across, 1.0, 0.0), axis=0, keepdims=True)
    place_down = jnp.sum(jnp.where(across > down, 1.0, 0.0), axis=1, keepdims=True)
    stands = place_down == lane
    order = jnp.sum(jnp.where(stands, lane.T, 0.0), axis=0, keepdims=True)
    sorted_tiles = jnp.sum(jnp.where(stands, tiles_across.T, 0.0), axis=0, keepdims=True)
    place_ref[...] = jnp.broadcast_to(place_across, place_ref.shape).astype(jnp.int32)
    order_ref[...] = order.astype(jnp.int32)
    tiles_ref[...] = sorted_tiles.astype(jnp.int32)
    nq, nk = cand_ref.shape
    cand = jnp.concatenate([cand_ref[...], jnp.zeros((nq, LANES - nk), jnp.int32)], axis=1)
    block, at = lax.shift_right_logical(cand, 7), jnp.bitwise_and(cand, LANES - 1)
    store = jnp.zeros((nq, LANES), jnp.int32)
    for b in range(home_ref.shape[0]):
        line = jnp.broadcast_to(home_ref[b : b + 1, :], (nq, LANES))
        store = jnp.where(block == b, jnp.take_along_axis(line, at, axis=1), store)
    shard_ref[...] = store // total
    local_ref[...] = store % total


def prepare(counts, home, candidates):
    nq = candidates.shape[0]
    index = jax.ShapeDtypeStruct((nq, LANES), jnp.int32)
    line = jax.ShapeDtypeStruct((1, LANES), jnp.int32)
    return pl.pallas_call(
        prepare_kernel,
        out_shape=[index, index, jax.ShapeDtypeStruct((8, LANES), jnp.int32), line, line],
        compiler_params=pltpu.CompilerParams(vmem_limit_bytes=58 * MIB),
        cost_estimate=pl.CostEstimate(flops=10**8, bytes_accessed=10**5, transcendentals=0),
        name="prepare",
    )(counts.reshape(1, -1), home.reshape(-1, LANES), candidates)


def maxsim_kernel(
    count_ref, order_ref, tiles_ref, g_ref, p_ref, place_ref, o_ref, best_ref, lhs_ref, table_ref, *, width, tokens, mine
):
    count, length, dim = p_ref.shape
    columns = g_ref.shape[0]
    best_ref[count:, :] = jnp.zeros((best_ref.shape[0] - count, columns), jnp.float32)

    def one(g, carry):
        at = pl.multiple_of(g * PER, PER)
        for tiles in range(1, length // ROWS + 1):
            rows = tiles * ROWS

            @pl.when(tiles_ref[0, at] == tiles)
            def _(rows=rows):
                index = lax.broadcasted_iota(jnp.int32, (rows, dim), 0)
                for i in range(PER):
                    p = order_ref[0, at + i]
                    block = p_ref[p, :rows, :].astype(jnp.float32)
                    block = jnp.where(index < count_ref[p], block, block[0:1])
                    lhs_ref[i * rows : (i + 1) * rows, :] = block.astype(lhs_ref.dtype)
                lhs = lhs_ref[: PER * rows, :]
                for col in range(0, columns, width):
                    dots = lax.dot_general(
                        lhs, g_ref[col : col + width, :], (((1,), (1,)), ((), ())), preferred_element_type=jnp.float32
                    )
                    best = jnp.max(dots.reshape(PER, rows // 8, 8, width), axis=1)
                    best_ref[pl.ds(at, PER), col : col + width] = jnp.max(best, axis=1)

        return carry

    lax.fori_loop(0, count // PER, one, 0)
    nq = columns // tokens
    owner = lax.broadcasted_iota(jnp.int32, (nq, columns), 1) // tokens
    pick = (owner == lax.broadcasted_iota(jnp.int32, (nq, columns), 0)).astype(jnp.bfloat16)
    rest = best_ref[...]
    total = jnp.zeros((nq, best_ref.shape[0]), jnp.float32)
    for _ in range(3):
        part = rest.astype(jnp.bfloat16)
        rest = rest - part.astype(jnp.float32)
        total += lax.dot_general(pick, part, (((1,), (1,)), ((), ())), preferred_element_type=jnp.float32)
    place = jnp.broadcast_to(place_ref[0:1, :], total.shape)
    table_ref[...] = jnp.take_along_axis(total, place, axis=1)
    copies = o_ref.shape[0] // nq
    for j in range(mine):
        lines = table_ref[pl.ds(j, nq // mine, stride=mine), :]
        for k in range(copies):
            o_ref[pl.ds(k * mine + j, nq // mine, stride=copies * mine), :] = lines


def maxsim(counts, order, tiles, gathered, passages, places, tokens, mine, copies, width=512):
    columns, dim = gathered.shape
    count, length, _ = passages.shape
    nq = columns // tokens
    vmem = pl.BlockSpec(memory_space=pltpu.VMEM)
    smem = pl.BlockSpec(memory_space=pltpu.SMEM)
    return pl.pallas_call(
        functools.partial(maxsim_kernel, width=width, tokens=tokens, mine=mine),
        in_specs=[smem, smem, smem, vmem, vmem, vmem],
        out_specs=vmem,
        out_shape=jax.ShapeDtypeStruct((copies * nq, LANES), jnp.float32),
        scratch_shapes=[
            pltpu.VMEM((LANES, columns), jnp.float32),
            pltpu.VMEM((PER * length, dim), jnp.bfloat16),
            pltpu.VMEM((nq, LANES), jnp.float32),
        ],
        compiler_params=pltpu.CompilerParams(vmem_limit_bytes=40 * MIB),
        cost_estimate=pl.CostEstimate(
            flops=2 * columns * count * length * dim, bytes_accessed=2 * passages.size, transcendentals=0
        ),
        name="maxsim",
    )(counts, order, tiles, gathered, passages, places)


def merge_kernel(r_ref, o_ref):
    tiles = r_ref.shape[1] // NPROBE
    nt = o_ref.shape[2]
    for tile in range(tiles):
        top = fold_sublanes([r_ref[:, rank * tiles + tile, :] for rank in range(NPROBE)])
        four = jnp.concatenate([t[0:1] for t in top], axis=0)
        for i in range(LANES // nt):
            o_ref[tile * (LANES // nt) + i] = four[:, i * nt : (i + 1) * nt]


def merge(received, rows, nq, nt):
    cents = received.shape[0]
    return pl.pallas_call(
        merge_kernel,
        grid=(1,),
        in_specs=[pl.BlockSpec((cents, rows, LANES), lambda i: (0, 0, 0))],
        out_specs=pl.BlockSpec((nq, NPROBE, nt), lambda i: (0, 0, 0)),
        out_shape=jax.ShapeDtypeStruct((nq, NPROBE, nt), jnp.float32),
        compiler_params=pltpu.CompilerParams(vmem_limit_bytes=16 * MIB),
        name="merge",
    )(received)


def lookup_kernel(r_ref, shard_ref, local_ref, o_ref):
    nq, nk = o_ref.shape
    home, local = shard_ref[...], local_ref[...]
    score = jnp.zeros(home.shape, jnp.float32)
    for s in range(r_ref.shape[0] // nq):
        table = r_ref[s * nq : (s + 1) * nq, :]
        score = jnp.where(home == s, jnp.take_along_axis(table, local, axis=1), score)
    o_ref[...] = score[:, :nk]


def lookup(received, shard_index, local_index, nq, nk):
    return pl.pallas_call(
        lookup_kernel,
        out_shape=jax.ShapeDtypeStruct((nq, nk), jnp.float32),
        compiler_params=pltpu.CompilerParams(vmem_limit_bytes=16 * MIB),
        name="lookup",
    )(received, shard_index, local_index)


def spread(block, copies):
    return jnp.broadcast_to(block[None], (copies,) + block.shape).reshape((-1,) + block.shape[1:])


def body(queries, centroids, passages, counts, home, candidates):
    nq, nt, dim = queries.shape
    nk = candidates.shape[1]
    shards, cents = lax.axis_size("shard"), lax.axis_size("cent")
    mine = nq // cents
    tokens = queries.reshape(nq * nt, dim)
    own = lax.dynamic_slice_in_dim(tokens, lax.axis_index("cent") * mine * nt, mine * nt, 0)
    gathered = lax.all_to_all(spread(own, shards), "shard", 0, 0, tiled=True)
    rows = NPROBE * nq * nt // LANES
    lists = probe(tokens, centroids, SENT)
    shard_index, local_index, places, order, tiles = prepare(counts, home, candidates)
    gathered, lists, places, order, tiles = lax.optimization_barrier((gathered, lists, places, order, tiles))
    received = pltpu.with_memory_space_constraint(lax.all_gather(lists, "cent"), pltpu.HBM)
    table = maxsim(counts, order, tiles, gathered, passages, places, nt, mine, cents)
    returned = lax.all_to_all(table, ("shard", "cent"), 0, 0, tiled=True)
    probe_scores = merge(received, rows, nq, nt)
    returned, probe_scores = lax.optimization_barrier((returned, probe_scores))
    passage_scores = lookup(returned, shard_index, local_index, nq, nk)
    return jnp.transpose(probe_scores, (0, 2, 1)), passage_scores


def solution(mesh):
    in_specs = (
        P("shard", None, None),
        P("cent", None),
        P("shard", None, None),
        P("shard"),
        P(),
        P("shard", "cent"),
    )
    out_specs = (P("shard", None, None), P("shard", "cent"))
    return jax.shard_map(body, mesh=mesh, in_specs=in_specs, out_specs=out_specs, check_vma=False)
```

```python
import functools

import jax
import jax.numpy as jnp
from jax import lax
from jax.experimental import pallas as pl
from jax.experimental.pallas import tpu as pltpu
from jax.sharding import PartitionSpec as P

NPROBE = 4
LANES = 128
MIB = 1024 * 1024
LEVELS = 3
GROUP = 16
ROWS = 32
PER = 16
FIRST = 7


def insert(running, x):
    out = []
    for rank, held in enumerate(running):
        out.append(jnp.maximum(held, x))
        if rank + 1 < len(running):
            x = jnp.minimum(held, x)
    return out


def streams(levels):
    return [2] * levels + [NPROBE]


def feed(xs, lists):
    for level in range(len(lists) - 1):
        half = len(xs) // 2
        losers = [jnp.minimum(a, b) for a, b in zip(xs[:half], xs[half:])]
        xs = [jnp.maximum(a, b) for a, b in zip(xs[:half], xs[half:])]
        for x in losers:
            lists[level] = insert(lists[level], x)
    for x in xs:
        lists[-1] = insert(lists[-1], x)


def merge_lists(a, b):
    m = [jnp.maximum(a[i], b[NPROBE - 1 - i]) for i in range(NPROBE)]
    for i, j in ((0, 2), (1, 3), (0, 1), (2, 3)):
        m[i], m[j] = jnp.maximum(m[i], m[j]), jnp.minimum(m[i], m[j])
    return m


def fold_sublanes(lists):
    for shift in (4, 2, 1):
        lists = merge_lists(lists, [pltpu.roll(t, shift, 0) for t in lists])
    return lists


def probe_kernel(q_ref, c_ref, *refs):
    before_ref = refs[0] if len(refs) > 2 else None
    o_ref, list_ref = refs[-2:]
    step = pl.program_id(0)
    kept = streams(LEVELS)
    nq = q_ref.shape[0]

    @pl.when(step == 0)
    def _():
        list_ref[...] = jnp.full(list_ref.shape, -jnp.inf, jnp.float32)

    scores = lax.dot_general(
        c_ref[...], q_ref[...], (((1,), (1,)), ((), ())), preferred_element_type=jnp.float32
    )
    for col in range(0, nq, LANES):
        at = 0
        lists = []
        for k in kept:
            lists.append([list_ref[at + a, :, col : col + LANES] for a in range(k)])
            at += k
        for row in range(0, scores.shape[0], 8 * GROUP):
            feed([scores[row + 8 * r : row + 8 * r + 8, col : col + LANES] for r in range(GROUP)], lists)
        at = 0
        for held in lists:
            for a, t in enumerate(held):
                list_ref[at + a, :, col : col + LANES] = t
            at += len(held)

    @pl.when(step == pl.num_programs(0) - 1)
    def _():
        for tile in range(nq // LANES):
            at = 0
            lists = []
            for k in kept:
                lists.append([list_ref[at + a, :, tile * LANES : (tile + 1) * LANES] for a in range(k)])
                at += k
            top = lists[-1]
            for held in lists[:-1]:
                for x in held:
                    top = insert(top, x)
            top = fold_sublanes(top)
            at_rows = [rank * (nq // LANES) + tile for rank in range(NPROBE)]
            top = [t[0:1] for t in top]
            if before_ref is not None:
                top = merge_lists(top, [before_ref[row : row + 1, :] for row in at_rows])
            for rank, row in enumerate(at_rows):
                o_ref[row : row + 1, :] = top[rank]


def probe(queries, centroids, before, first, steps, block=4096):
    nq, dim = queries.shape
    total = steps * block
    rows = NPROBE * nq // LANES
    return pl.pallas_call(
        probe_kernel,
        grid=(steps,),
        in_specs=[
            pl.BlockSpec((nq, dim), lambda i: (0, 0)),
            pl.BlockSpec((block, dim), lambda i: (first + i, 0)),
        ]
        + [pl.BlockSpec((rows, LANES), lambda i: (0, 0))] * len(before),
        out_specs=pl.BlockSpec((rows, LANES), lambda i: (0, 0)),
        out_shape=jax.ShapeDtypeStruct((rows, LANES), jnp.float32),
        scratch_shapes=[pltpu.VMEM((sum(streams(LEVELS)), 8, nq), jnp.float32)],
        compiler_params=pltpu.CompilerParams(vmem_limit_bytes=24 * MIB),
        cost_estimate=pl.CostEstimate(
            flops=4 * nq * total * dim, bytes_accessed=2 * total * dim, transcendentals=0
        ),
        name=f"probe_{first}",
    )(queries, centroids, *before)


def prepare_kernel(count_ref, home_ref, cand_ref, shard_ref, local_ref, place_ref, order_ref, tiles_ref):
    total = count_ref.shape[1]
    counts = jnp.concatenate([count_ref[...], jnp.full((1, LANES - total), 1 - ROWS, jnp.int32)], axis=1)
    tiles = lax.shift_right_arithmetic(counts + (ROWS - 1), ROWS.bit_length() - 1)
    lane = lax.broadcasted_iota(jnp.int32, (LANES, LANES), 1).astype(jnp.float32)
    tiles_across = jnp.broadcast_to(tiles.astype(jnp.float32), (LANES, LANES))
    across = tiles_across * LANES - lane
    down = across.T
    place_across = jnp.sum(jnp.where(down > across, 1.0, 0.0), axis=0, keepdims=True)
    place_down = jnp.sum(jnp.where(across > down, 1.0, 0.0), axis=1, keepdims=True)
    stands = place_down == lane
    order = jnp.sum(jnp.where(stands, lane.T, 0.0), axis=0, keepdims=True)
    sorted_tiles = jnp.sum(jnp.where(stands, tiles_across.T, 0.0), axis=0, keepdims=True)
    place_ref[...] = jnp.broadcast_to(place_across, place_ref.shape).astype(jnp.int32)
    order_ref[...] = order.astype(jnp.int32)
    tiles_ref[...] = sorted_tiles.astype(jnp.int32)
    nq, nk = cand_ref.shape
    cand = jnp.concatenate([cand_ref[...], jnp.zeros((nq, LANES - nk), jnp.int32)], axis=1)
    block, at = lax.shift_right_logical(cand, 7), jnp.bitwise_and(cand, LANES - 1)
    store = jnp.zeros((nq, LANES), jnp.int32)
    for b in range(home_ref.shape[0]):
        line = jnp.broadcast_to(home_ref[b : b + 1, :], (nq, LANES))
        store = jnp.where(block == b, jnp.take_along_axis(line, at, axis=1), store)
    shard_ref[...] = store // total
    local_ref[...] = store % total


def prepare(counts, home, candidates):
    nq = candidates.shape[0]
    index = jax.ShapeDtypeStruct((nq, LANES), jnp.int32)
    line = jax.ShapeDtypeStruct((1, LANES), jnp.int32)
    return pl.pallas_call(
        prepare_kernel,
        out_shape=[index, index, jax.ShapeDtypeStruct((8, LANES), jnp.int32), line, line],
        compiler_params=pltpu.CompilerParams(vmem_limit_bytes=58 * MIB),
        cost_estimate=pl.CostEstimate(flops=10**8, bytes_accessed=10**5, transcendentals=0),
        name="prepare",
    )(counts.reshape(1, -1), home.reshape(-1, LANES), candidates)


def maxsim_kernel(count_ref, order_ref, tiles_ref, g_ref, p_ref, place_ref, o_ref, best_ref, lhs_ref, *, width, tokens):
    count, length, dim = p_ref.shape
    columns = g_ref.shape[0]
    best_ref[count:, :] = jnp.zeros((best_ref.shape[0] - count, columns), jnp.float32)

    def one(g, carry):
        at = pl.multiple_of(g * PER, PER)
        for tiles in range(1, length // ROWS + 1):
            rows = tiles * ROWS

            @pl.when(tiles_ref[0, at] == tiles)
            def _(rows=rows):
                index = lax.broadcasted_iota(jnp.int32, (rows, dim), 0)
                for i in range(PER):
                    p = order_ref[0, at + i]
                    block = p_ref[p, :rows, :].astype(jnp.float32)
                    block = jnp.where(index < count_ref[p], block, block[0:1])
                    lhs_ref[i * rows : (i + 1) * rows, :] = block.astype(lhs_ref.dtype)
                lhs = lhs_ref[: PER * rows, :]
                for col in range(0, columns, width):
                    dots = lax.dot_general(
                        lhs, g_ref[col : col + width, :], (((1,), (1,)), ((), ())), preferred_element_type=jnp.float32
                    )
                    best = jnp.max(dots.reshape(PER, rows // 8, 8, width), axis=1)
                    best_ref[pl.ds(at, PER), col : col + width] = jnp.max(best, axis=1)

        return carry

    lax.fori_loop(0, count // PER, one, 0)
    nq = o_ref.shape[0]
    owner = lax.broadcasted_iota(jnp.int32, (nq, columns), 1) // tokens
    pick = (owner == lax.broadcasted_iota(jnp.int32, (nq, columns), 0)).astype(jnp.bfloat16)
    rest = best_ref[...]
    total = jnp.zeros((nq, best_ref.shape[0]), jnp.float32)
    for _ in range(3):
        part = rest.astype(jnp.bfloat16)
        rest = rest - part.astype(jnp.float32)
        total += lax.dot_general(pick, part, (((1,), (1,)), ((), ())), preferred_element_type=jnp.float32)
    place = jnp.broadcast_to(place_ref[0:1, :], total.shape)
    o_ref[...] = jnp.take_along_axis(total, place, axis=1)


def maxsim(counts, order, tiles, gathered, passages, places, tokens, width=512):
    columns, dim = gathered.shape
    count, length, _ = passages.shape
    nq = columns // tokens
    vmem = pl.BlockSpec(memory_space=pltpu.VMEM)
    smem = pl.BlockSpec(memory_space=pltpu.SMEM)
    return pl.pallas_call(
        functools.partial(maxsim_kernel, width=width, tokens=tokens),
        in_specs=[smem, smem, smem, vmem, vmem, vmem],
        out_specs=vmem,
        out_shape=jax.ShapeDtypeStruct((nq, LANES), jnp.float32),
        scratch_shapes=[pltpu.VMEM((LANES, columns), jnp.float32), pltpu.VMEM((PER * length, dim), jnp.bfloat16)],
        compiler_params=pltpu.CompilerParams(vmem_limit_bytes=40 * MIB),
        cost_estimate=pl.CostEstimate(
            flops=2 * columns * count * length * dim, bytes_accessed=2 * passages.size, transcendentals=0
        ),
        name="maxsim",
    )(counts, order, tiles, gathered, passages, places)


def finish_kernel(r_ref, shard_ref, local_ref, probe_ref, score_ref, *, shards, cents):
    lines = r_ref.shape[0] // cents
    half = shard_ref.shape[0] // 2
    nk = score_ref.shape[1]
    for j in range(2):
        home = shard_ref[pl.ds(j, half, stride=2), :]
        local = local_ref[pl.ds(j, half, stride=2), :]
        score = jnp.zeros(home.shape, jnp.float32)
        for s in range(shards):
            table = r_ref[pl.ds(2 * s + j, cents, stride=lines), :]
            score = jnp.where(home == s, jnp.take_along_axis(table, local, axis=1), score)
        score_ref[pl.ds(j, half, stride=2), :] = score[:, :nk]
    first = 2 * shards
    tiles = (lines - first) // NPROBE
    nt = probe_ref.shape[2]
    for tile in range(tiles):
        top = fold_sublanes(
            [r_ref[pl.ds(first + rank * tiles + tile, cents, stride=lines), :] for rank in range(NPROBE)]
        )
        four = jnp.concatenate([t[0:1] for t in top], axis=0)
        for i in range(LANES // nt):
            probe_ref[tile * (LANES // nt) + i] = four[:, i * nt : (i + 1) * nt]


def finish(received, shard_index, local_index, shards, cents, nq, nt, nk):
    return pl.pallas_call(
        functools.partial(finish_kernel, shards=shards, cents=cents),
        out_shape=[
            jax.ShapeDtypeStruct((nq, NPROBE, nt), jnp.float32),
            jax.ShapeDtypeStruct((nq, nk), jnp.float32),
        ],
        compiler_params=pltpu.CompilerParams(vmem_limit_bytes=16 * MIB),
        name="finish",
    )(received, shard_index, local_index)


def spread(block, copies):
    return jnp.broadcast_to(block[None], (copies,) + block.shape).reshape((-1,) + block.shape[1:])


def body(queries, centroids, passages, counts, home, candidates):
    nq, nt, dim = queries.shape
    nk = candidates.shape[1]
    shards, cents = lax.axis_size("shard"), lax.axis_size("cent")
    mine = nq // cents
    tokens = queries.reshape(nq * nt, dim)
    own = lax.dynamic_slice_in_dim(tokens, lax.axis_index("cent") * mine * nt, mine * nt, 0)
    gathered = lax.all_to_all(spread(own, shards), "shard", 0, 0, tiled=True)
    blocks = centroids.shape[0] // 4096
    centroids = pltpu.with_memory_space_constraint(centroids, pltpu.HBM)
    lists = probe(tokens, centroids, (), 0, FIRST)
    shard_index, local_index, places, order, tiles = prepare(counts, home, candidates)
    gathered, lists, places, order, tiles = lax.optimization_barrier((gathered, lists, places, order, tiles))
    table = maxsim(counts, order, tiles, gathered, passages, places, nt)
    table, lists = lax.optimization_barrier((table, lists))
    returned = lax.all_to_all(table, "shard", 0, 0, tiled=True)
    lists = probe(tokens, centroids, (lists,), FIRST, blocks - FIRST)
    final = spread(jnp.concatenate([returned, lists], axis=0), cents)
    received = lax.all_to_all(final, "cent", 0, 0, tiled=True)
    probe_scores, passage_scores = finish(received, shard_index, local_index, shards, cents, nq, nt, nk)
    return jnp.transpose(probe_scores, (0, 2, 1)), passage_scores


def solution(mesh):
    in_specs = (
        P("shard", None, None),
        P("cent", None),
        P("shard", None, None),
        P("shard"),
        P(),
        P("shard", "cent"),
    )
    out_specs = (P("shard", None, None), P("shard", "cent"))
    return jax.shard_map(body, mesh=mesh, in_specs=in_specs, out_specs=out_specs, check_vma=False)
```

```python
import functools

import jax
import jax.numpy as jnp
from jax import lax
from jax.experimental import pallas as pl
from jax.experimental.pallas import tpu as pltpu
from jax.sharding import PartitionSpec as P

NPROBE = 4
LANES = 128
MIB = 1024 * 1024
LEVELS = 3
GROUP = 16
ROWS = 32
PER = 16
FIRST = 7


def insert(running, x):
    out = []
    for rank, held in enumerate(running):
        out.append(jnp.maximum(held, x))
        if rank + 1 < len(running):
            x = jnp.minimum(held, x)
    return out


def streams(levels):
    return [2] * levels + [NPROBE]


def feed(xs, lists):
    for level in range(len(lists) - 1):
        half = len(xs) // 2
        losers = [jnp.minimum(a, b) for a, b in zip(xs[:half], xs[half:])]
        xs = [jnp.maximum(a, b) for a, b in zip(xs[:half], xs[half:])]
        for x in losers:
            lists[level] = insert(lists[level], x)
    for x in xs:
        lists[-1] = insert(lists[-1], x)


def merge_lists(a, b):
    m = [jnp.maximum(a[i], b[NPROBE - 1 - i]) for i in range(NPROBE)]
    for i, j in ((0, 2), (1, 3), (0, 1), (2, 3)):
        m[i], m[j] = jnp.maximum(m[i], m[j]), jnp.minimum(m[i], m[j])
    return m


def fold_sublanes(lists):
    for shift in (4, 2, 1):
        lists = merge_lists(lists, [pltpu.roll(t, shift, 0) for t in lists])
    return lists


def probe_kernel(q_ref, c_ref, *refs):
    before_ref = refs[0] if len(refs) > 2 else None
    o_ref, list_ref = refs[-2:]
    step = pl.program_id(0)
    kept = streams(LEVELS)
    nq = q_ref.shape[0]

    @pl.when(step == 0)
    def _():
        list_ref[...] = jnp.full(list_ref.shape, -jnp.inf, jnp.float32)

    scores = lax.dot_general(
        c_ref[...], q_ref[...], (((1,), (1,)), ((), ())), preferred_element_type=jnp.float32
    )
    for col in range(0, nq, LANES):
        at = 0
        lists = []
        for k in kept:
            lists.append([list_ref[at + a, :, col : col + LANES] for a in range(k)])
            at += k
        for row in range(0, scores.shape[0], 8 * GROUP):
            feed([scores[row + 8 * r : row + 8 * r + 8, col : col + LANES] for r in range(GROUP)], lists)
        at = 0
        for held in lists:
            for a, t in enumerate(held):
                list_ref[at + a, :, col : col + LANES] = t
            at += len(held)

    @pl.when(step == pl.num_programs(0) - 1)
    def _():
        for tile in range(nq // LANES):
            at = 0
            lists = []
            for k in kept:
                lists.append([list_ref[at + a, :, tile * LANES : (tile + 1) * LANES] for a in range(k)])
                at += k
            top = lists[-1]
            for held in lists[:-1]:
                for x in held:
                    top = insert(top, x)
            top = fold_sublanes(top)
            at_rows = [rank * (nq // LANES) + tile for rank in range(NPROBE)]
            top = [t[0:1] for t in top]
            if before_ref is not None:
                top = merge_lists(top, [before_ref[row : row + 1, :] for row in at_rows])
            for rank, row in enumerate(at_rows):
                o_ref[row : row + 1, :] = top[rank]


def probe(queries, centroids, before, first, steps, block=4096):
    nq, dim = queries.shape
    total = steps * block
    rows = NPROBE * nq // LANES
    return pl.pallas_call(
        probe_kernel,
        grid=(steps,),
        in_specs=[
            pl.BlockSpec((nq, dim), lambda i: (0, 0)),
            pl.BlockSpec((block, dim), lambda i: (first + i, 0)),
        ]
        + [pl.BlockSpec((rows, LANES), lambda i: (0, 0))] * len(before),
        out_specs=pl.BlockSpec((rows, LANES), lambda i: (0, 0)),
        out_shape=jax.ShapeDtypeStruct((rows, LANES), jnp.float32),
        scratch_shapes=[pltpu.VMEM((sum(streams(LEVELS)), 8, nq), jnp.float32)],
        compiler_params=pltpu.CompilerParams(vmem_limit_bytes=58 * MIB),
        cost_estimate=pl.CostEstimate(
            flops=4 * nq * total * dim, bytes_accessed=2 * total * dim, transcendentals=0
        ),
        name=f"probe_{first}",
    )(queries, centroids, *before)


def prepare_kernel(count_ref, home_ref, cand_ref, shard_ref, local_ref, place_ref, order_ref, tiles_ref):
    total = count_ref.shape[1]
    counts = jnp.concatenate([count_ref[...], jnp.full((1, LANES - total), 1 - ROWS, jnp.int32)], axis=1)
    tiles = lax.shift_right_arithmetic(counts + (ROWS - 1), ROWS.bit_length() - 1)
    lane = lax.broadcasted_iota(jnp.int32, (LANES, LANES), 1).astype(jnp.float32)
    tiles_across = jnp.broadcast_to(tiles.astype(jnp.float32), (LANES, LANES))
    across = tiles_across * LANES - lane
    down = across.T
    place_across = jnp.sum(jnp.where(down > across, 1.0, 0.0), axis=0, keepdims=True)
    place_down = jnp.sum(jnp.where(across > down, 1.0, 0.0), axis=1, keepdims=True)
    stands = place_down == lane
    order = jnp.sum(jnp.where(stands, lane.T, 0.0), axis=0, keepdims=True)
    sorted_tiles = jnp.sum(jnp.where(stands, tiles_across.T, 0.0), axis=0, keepdims=True)
    place_ref[...] = jnp.broadcast_to(place_across, place_ref.shape).astype(jnp.int32)
    order_ref[...] = order.astype(jnp.int32)
    tiles_ref[...] = sorted_tiles.astype(jnp.int32)
    nq, nk = cand_ref.shape
    cand = jnp.concatenate([cand_ref[...], jnp.zeros((nq, LANES - nk), jnp.int32)], axis=1)
    block, at = lax.shift_right_logical(cand, 7), jnp.bitwise_and(cand, LANES - 1)
    store = jnp.zeros((nq, LANES), jnp.int32)
    for b in range(home_ref.shape[0]):
        line = jnp.broadcast_to(home_ref[b : b + 1, :], (nq, LANES))
        store = jnp.where(block == b, jnp.take_along_axis(line, at, axis=1), store)
    shard_ref[...] = store // total
    local_ref[...] = store % total


def prepare(counts, home, candidates):
    nq = candidates.shape[0]
    index = jax.ShapeDtypeStruct((nq, LANES), jnp.int32)
    line = jax.ShapeDtypeStruct((1, LANES), jnp.int32)
    return pl.pallas_call(
        prepare_kernel,
        out_shape=[index, index, jax.ShapeDtypeStruct((8, LANES), jnp.int32), line, line],
        compiler_params=pltpu.CompilerParams(vmem_limit_bytes=58 * MIB),
        cost_estimate=pl.CostEstimate(flops=10**8, bytes_accessed=10**5, transcendentals=0),
        name="prepare",
    )(counts.reshape(1, -1), home.reshape(-1, LANES), candidates)


def maxsim_kernel(count_ref, order_ref, tiles_ref, g_ref, p_ref, place_ref, o_ref, best_ref, lhs_ref, *, width, tokens):
    count, length, dim = p_ref.shape
    columns = g_ref.shape[0]
    best_ref[count:, :] = jnp.zeros((best_ref.shape[0] - count, columns), jnp.float32)

    def one(g, carry):
        at = pl.multiple_of(g * PER, PER)
        for tiles in range(1, length // ROWS + 1):
            rows = tiles * ROWS

            @pl.when(tiles_ref[0, at] == tiles)
            def _(rows=rows):
                index = lax.broadcasted_iota(jnp.int32, (rows, dim), 0)
                for i in range(PER):
                    p = order_ref[0, at + i]
                    block = p_ref[p, :rows, :].astype(jnp.float32)
                    block = jnp.where(index < count_ref[p], block, block[0:1])
                    lhs_ref[i * rows : (i + 1) * rows, :] = block.astype(lhs_ref.dtype)
                lhs = lhs_ref[: PER * rows, :]
                for col in range(0, columns, width):
                    dots = lax.dot_general(
                        lhs, g_ref[col : col + width, :], (((1,), (1,)), ((), ())), preferred_element_type=jnp.float32
                    )
                    best = jnp.max(dots.reshape(PER, rows // 8, 8, width), axis=1)
                    best_ref[pl.ds(at, PER), col : col + width] = jnp.max(best, axis=1)

        return carry

    lax.fori_loop(0, count // PER, one, 0)
    nq = o_ref.shape[0]
    owner = lax.broadcasted_iota(jnp.int32, (nq, columns), 1) // tokens
    pick = (owner == lax.broadcasted_iota(jnp.int32, (nq, columns), 0)).astype(jnp.bfloat16)
    rest = best_ref[...]
    total = jnp.zeros((nq, best_ref.shape[0]), jnp.float32)
    for _ in range(3):
        part = rest.astype(jnp.bfloat16)
        rest = rest - part.astype(jnp.float32)
        total += lax.dot_general(pick, part, (((1,), (1,)), ((), ())), preferred_element_type=jnp.float32)
    place = jnp.broadcast_to(place_ref[0:1, :], total.shape)
    o_ref[...] = jnp.take_along_axis(total, place, axis=1)


def maxsim(counts, order, tiles, gathered, passages, places, tokens, width=512):
    columns, dim = gathered.shape
    count, length, _ = passages.shape
    nq = columns // tokens
    vmem = pl.BlockSpec(memory_space=pltpu.VMEM)
    smem = pl.BlockSpec(memory_space=pltpu.SMEM)
    return pl.pallas_call(
        functools.partial(maxsim_kernel, width=width, tokens=tokens),
        in_specs=[smem, smem, smem, vmem, vmem, vmem],
        out_specs=vmem,
        out_shape=jax.ShapeDtypeStruct((nq, LANES), jnp.float32),
        scratch_shapes=[pltpu.VMEM((LANES, columns), jnp.float32), pltpu.VMEM((PER * length, dim), jnp.bfloat16)],
        compiler_params=pltpu.CompilerParams(vmem_limit_bytes=40 * MIB),
        cost_estimate=pl.CostEstimate(
            flops=2 * columns * count * length * dim, bytes_accessed=2 * passages.size, transcendentals=0
        ),
        name="maxsim",
    )(counts, order, tiles, gathered, passages, places)


def finish_kernel(r_ref, shard_ref, local_ref, probe_ref, score_ref, *, shards, cents):
    lines = r_ref.shape[0] // cents
    half = shard_ref.shape[0] // 2
    nk = score_ref.shape[1]
    for j in range(2):
        home = shard_ref[pl.ds(j, half, stride=2), :]
        local = local_ref[pl.ds(j, half, stride=2), :]
        score = jnp.zeros(home.shape, jnp.float32)
        for s in range(shards):
            table = r_ref[pl.ds(2 * s + j, cents, stride=lines), :]
            score = jnp.where(home == s, jnp.take_along_axis(table, local, axis=1), score)
        score_ref[pl.ds(j, half, stride=2), :] = score[:, :nk]
    first = 2 * shards
    tiles = (lines - first) // NPROBE
    nt = probe_ref.shape[2]
    for tile in range(tiles):
        top = fold_sublanes(
            [r_ref[pl.ds(first + rank * tiles + tile, cents, stride=lines), :] for rank in range(NPROBE)]
        )
        four = jnp.concatenate([t[0:1] for t in top], axis=0)
        for i in range(LANES // nt):
            probe_ref[tile * (LANES // nt) + i] = four[:, i * nt : (i + 1) * nt]


def finish(received, shard_index, local_index, shards, cents, nq, nt, nk):
    return pl.pallas_call(
        functools.partial(finish_kernel, shards=shards, cents=cents),
        out_shape=[
            jax.ShapeDtypeStruct((nq, NPROBE, nt), jnp.float32),
            jax.ShapeDtypeStruct((nq, nk), jnp.float32),
        ],
        compiler_params=pltpu.CompilerParams(vmem_limit_bytes=16 * MIB),
        name="finish",
    )(received, shard_index, local_index)


def spread(block, copies):
    return jnp.broadcast_to(block[None], (copies,) + block.shape).reshape((-1,) + block.shape[1:])


def body(queries, centroids, passages, counts, home, candidates):
    nq, nt, dim = queries.shape
    nk = candidates.shape[1]
    shards, cents = lax.axis_size("shard"), lax.axis_size("cent")
    mine = nq // cents
    tokens = queries.reshape(nq * nt, dim)
    own = lax.dynamic_slice_in_dim(tokens, lax.axis_index("cent") * mine * nt, mine * nt, 0)
    gathered = lax.all_to_all(spread(own, shards), "shard", 0, 0, tiled=True)
    blocks = centroids.shape[0] // 4096
    centroids = pltpu.with_memory_space_constraint(centroids, pltpu.HBM)
    lists = probe(tokens, centroids, (), 0, FIRST)
    shard_index, local_index, places, order, tiles = prepare(counts, home, candidates)
    gathered, lists, places, order, tiles = lax.optimization_barrier((gathered, lists, places, order, tiles))
    gathered = pltpu.with_memory_space_constraint(gathered, pltpu.HBM)
    table = maxsim(counts, order, tiles, gathered, passages, places, nt)
    table, lists = lax.optimization_barrier((table, lists))
    returned = lax.all_to_all(table, "shard", 0, 0, tiled=True)
    lists = probe(tokens, centroids, (lists,), FIRST, blocks - FIRST)
    final = spread(jnp.concatenate([returned, lists], axis=0), cents)
    received = lax.all_to_all(final, "cent", 0, 0, tiled=True)
    probe_scores, passage_scores = finish(received, shard_index, local_index, shards, cents, nq, nt, nk)
    return jnp.transpose(probe_scores, (0, 2, 1)), passage_scores


def solution(mesh):
    in_specs = (
        P("shard", None, None),
        P("cent", None),
        P("shard", None, None),
        P("shard"),
        P(),
        P("shard", "cent"),
    )
    out_specs = (P("shard", None, None), P("shard", "cent"))
    return jax.shard_map(body, mesh=mesh, in_specs=in_specs, out_specs=out_specs, check_vma=False)
```

```python
import functools

import jax
import jax.numpy as jnp
from jax import lax
from jax.experimental import pallas as pl
from jax.experimental.pallas import tpu as pltpu
from jax.sharding import PartitionSpec as P

NPROBE = 4
LANES = 128
MIB = 1024 * 1024
LEVELS = 3
GROUP = 16
ROWS = 32
PER = 16
FIRST = 6


def insert(running, x):
    out = []
    for rank, held in enumerate(running):
        out.append(jnp.maximum(held, x))
        if rank + 1 < len(running):
            x = jnp.minimum(held, x)
    return out


def streams(levels):
    return [2] * levels + [NPROBE]


def feed(xs, lists):
    for level in range(len(lists) - 1):
        half = len(xs) // 2
        losers = [jnp.minimum(a, b) for a, b in zip(xs[:half], xs[half:])]
        xs = [jnp.maximum(a, b) for a, b in zip(xs[:half], xs[half:])]
        for x in losers:
            lists[level] = insert(lists[level], x)
    for x in xs:
        lists[-1] = insert(lists[-1], x)


def merge_lists(a, b):
    m = [jnp.maximum(a[i], b[NPROBE - 1 - i]) for i in range(NPROBE)]
    for i, j in ((0, 2), (1, 3), (0, 1), (2, 3)):
        m[i], m[j] = jnp.maximum(m[i], m[j]), jnp.minimum(m[i], m[j])
    return m


def fold_sublanes(lists):
    for shift in (4, 2, 1):
        lists = merge_lists(lists, [pltpu.roll(t, shift, 0) for t in lists])
    return lists


def probe_kernel(q_ref, c_ref, *refs):
    before_ref = refs[0] if len(refs) > 2 else None
    o_ref, list_ref = refs[-2:]
    step = pl.program_id(0)
    kept = streams(LEVELS)
    nq = q_ref.shape[0]

    @pl.when(step == 0)
    def _():
        list_ref[...] = jnp.full(list_ref.shape, -jnp.inf, jnp.float32)

    scores = lax.dot_general(
        c_ref[...], q_ref[...], (((1,), (1,)), ((), ())), preferred_element_type=jnp.float32
    )
    for col in range(0, nq, LANES):
        at = 0
        lists = []
        for k in kept:
            lists.append([list_ref[at + a, :, col : col + LANES] for a in range(k)])
            at += k
        for row in range(0, scores.shape[0], 8 * GROUP):
            feed([scores[row + 8 * r : row + 8 * r + 8, col : col + LANES] for r in range(GROUP)], lists)
        at = 0
        for held in lists:
            for a, t in enumerate(held):
                list_ref[at + a, :, col : col + LANES] = t
            at += len(held)

    @pl.when(step == pl.num_programs(0) - 1)
    def _():
        for tile in range(nq // LANES):
            at = 0
            lists = []
            for k in kept:
                lists.append([list_ref[at + a, :, tile * LANES : (tile + 1) * LANES] for a in range(k)])
                at += k
            top = lists[-1]
            for held in lists[:-1]:
                for x in held:
                    top = insert(top, x)
            top = fold_sublanes(top)
            at_rows = [rank * (nq // LANES) + tile for rank in range(NPROBE)]
            top = [t[0:1] for t in top]
            if before_ref is not None:
                top = merge_lists(top, [before_ref[row : row + 1, :] for row in at_rows])
            for rank, row in enumerate(at_rows):
                o_ref[row : row + 1, :] = top[rank]


def probe(queries, centroids, before, first, steps, block=4096):
    nq, dim = queries.shape
    total = steps * block
    rows = NPROBE * nq // LANES
    return pl.pallas_call(
        probe_kernel,
        grid=(steps,),
        in_specs=[
            pl.BlockSpec((nq, dim), lambda i: (0, 0)),
            pl.BlockSpec((block, dim), lambda i: (first + i, 0)),
        ]
        + [pl.BlockSpec((rows, LANES), lambda i: (0, 0))] * len(before),
        out_specs=pl.BlockSpec((rows, LANES), lambda i: (0, 0)),
        out_shape=jax.ShapeDtypeStruct((rows, LANES), jnp.float32),
        scratch_shapes=[pltpu.VMEM((sum(streams(LEVELS)), 8, nq), jnp.float32)],
        compiler_params=pltpu.CompilerParams(vmem_limit_bytes=58 * MIB),
        cost_estimate=pl.CostEstimate(
            flops=4 * nq * total * dim, bytes_accessed=2 * total * dim, transcendentals=0
        ),
        name=f"probe_{first}",
    )(queries, centroids, *before)


def prepare_kernel(count_ref, home_ref, cand_ref, shard_ref, local_ref, place_ref, order_ref, tiles_ref):
    total = count_ref.shape[1]
    counts = jnp.concatenate([count_ref[...], jnp.full((1, LANES - total), 1 - ROWS, jnp.int32)], axis=1)
    tiles = lax.shift_right_arithmetic(counts + (ROWS - 1), ROWS.bit_length() - 1)
    lane = lax.broadcasted_iota(jnp.int32, (LANES, LANES), 1).astype(jnp.float32)
    tiles_across = jnp.broadcast_to(tiles.astype(jnp.float32), (LANES, LANES))
    across = tiles_across * LANES - lane
    down = across.T
    place_across = jnp.sum(jnp.where(down > across, 1.0, 0.0), axis=0, keepdims=True)
    place_down = jnp.sum(jnp.where(across > down, 1.0, 0.0), axis=1, keepdims=True)
    stands = place_down == lane
    order = jnp.sum(jnp.where(stands, lane.T, 0.0), axis=0, keepdims=True)
    sorted_tiles = jnp.sum(jnp.where(stands, tiles_across.T, 0.0), axis=0, keepdims=True)
    place_ref[...] = jnp.broadcast_to(place_across, place_ref.shape).astype(jnp.int32)
    order_ref[...] = order.astype(jnp.int32)
    tiles_ref[...] = sorted_tiles.astype(jnp.int32)
    nq, nk = cand_ref.shape
    cand = jnp.concatenate([cand_ref[...], jnp.zeros((nq, LANES - nk), jnp.int32)], axis=1)
    block, at = lax.shift_right_logical(cand, 7), jnp.bitwise_and(cand, LANES - 1)
    store = jnp.zeros((nq, LANES), jnp.int32)
    for b in range(home_ref.shape[0]):
        line = jnp.broadcast_to(home_ref[b : b + 1, :], (nq, LANES))
        store = jnp.where(block == b, jnp.take_along_axis(line, at, axis=1), store)
    shard_ref[...] = store // total
    local_ref[...] = store % total


def prepare(counts, home, candidates):
    nq = candidates.shape[0]
    index = jax.ShapeDtypeStruct((nq, LANES), jnp.int32)
    line = jax.ShapeDtypeStruct((1, LANES), jnp.int32)
    return pl.pallas_call(
        prepare_kernel,
        out_shape=[index, index, jax.ShapeDtypeStruct((8, LANES), jnp.int32), line, line],
        compiler_params=pltpu.CompilerParams(vmem_limit_bytes=58 * MIB),
        cost_estimate=pl.CostEstimate(flops=10**8, bytes_accessed=10**5, transcendentals=0),
        name="prepare",
    )(counts.reshape(1, -1), home.reshape(-1, LANES), candidates)


def maxsim_kernel(count_ref, order_ref, tiles_ref, g_ref, p_ref, best_ref, lhs_ref, *, width):
    count, length, dim = p_ref.shape
    columns = g_ref.shape[0]

    def one(g, carry):
        at = pl.multiple_of(g * PER, PER)
        for tiles in range(1, length // ROWS + 1):
            rows = tiles * ROWS

            @pl.when(tiles_ref[0, at] == tiles)
            def _(rows=rows):
                index = lax.broadcasted_iota(jnp.int32, (rows, dim), 0)
                for i in range(PER):
                    p = order_ref[0, at + i]
                    block = p_ref[p, :rows, :].astype(jnp.float32)
                    block = jnp.where(index < count_ref[p], block, block[0:1])
                    lhs_ref[i * rows : (i + 1) * rows, :] = block.astype(lhs_ref.dtype)
                lhs = lhs_ref[: PER * rows, :]
                for col in range(0, columns, width):
                    dots = lax.dot_general(
                        lhs, g_ref[col : col + width, :], (((1,), (1,)), ((), ())), preferred_element_type=jnp.float32
                    )
                    best = jnp.max(dots.reshape(PER, rows // 8, 8, width), axis=1)
                    best_ref[pl.ds(at, PER), col : col + width] = jnp.max(best, axis=1)

        return carry

    lax.fori_loop(0, count // PER, one, 0)


def maxsim(counts, order, tiles, gathered, passages, width=512):
    columns, dim = gathered.shape
    count, length, _ = passages.shape
    vmem = pl.BlockSpec(memory_space=pltpu.VMEM)
    smem = pl.BlockSpec(memory_space=pltpu.SMEM)
    return pl.pallas_call(
        functools.partial(maxsim_kernel, width=width),
        in_specs=[smem, smem, smem, vmem, vmem],
        out_specs=vmem,
        out_shape=jax.ShapeDtypeStruct((count, columns), jnp.float32),
        scratch_shapes=[pltpu.VMEM((PER * length, dim), jnp.bfloat16)],
        compiler_params=pltpu.CompilerParams(vmem_limit_bytes=40 * MIB),
        cost_estimate=pl.CostEstimate(
            flops=2 * columns * count * length * dim, bytes_accessed=2 * passages.size, transcendentals=0
        ),
        name="maxsim",
    )(counts, order, tiles, gathered, passages)


def total_kernel(best_ref, place_ref, o_ref, *, tokens):
    count, columns = best_ref.shape
    nq = o_ref.shape[0]
    owner = lax.shift_right_logical(lax.broadcasted_iota(jnp.int32, (nq, columns), 1), tokens.bit_length() - 1)
    pick = (owner == lax.broadcasted_iota(jnp.int32, (nq, columns), 0)).astype(jnp.bfloat16)
    rest = jnp.concatenate([best_ref[...], jnp.zeros((LANES - count, columns), jnp.float32)], axis=0)
    total = jnp.zeros((nq, LANES), jnp.float32)
    for _ in range(3):
        part = rest.astype(jnp.bfloat16)
        rest = rest - part.astype(jnp.float32)
        total += lax.dot_general(pick, part, (((1,), (1,)), ((), ())), preferred_element_type=jnp.float32)
    place = jnp.broadcast_to(place_ref[0:1, :], total.shape)
    o_ref[...] = jnp.take_along_axis(total, place, axis=1)


def total_scores(best, places, tokens):
    nq = best.shape[1] // tokens
    return pl.pallas_call(
        functools.partial(total_kernel, tokens=tokens),
        out_shape=jax.ShapeDtypeStruct((nq, LANES), jnp.float32),
        compiler_params=pltpu.CompilerParams(vmem_limit_bytes=16 * MIB),
        cost_estimate=pl.CostEstimate(flops=10**8, bytes_accessed=best.size * 4, transcendentals=0),
        name="total",
    )(best, places)


def finish_kernel(r_ref, shard_ref, local_ref, probe_ref, score_ref, *, shards, cents):
    lines = r_ref.shape[0] // cents
    half = shard_ref.shape[0] // 2
    nk = score_ref.shape[1]
    for j in range(2):
        home = shard_ref[pl.ds(j, half, stride=2), :]
        local = local_ref[pl.ds(j, half, stride=2), :]
        score = jnp.zeros(home.shape, jnp.float32)
        for s in range(shards):
            table = r_ref[pl.ds(2 * s + j, cents, stride=lines), :]
            score = jnp.where(home == s, jnp.take_along_axis(table, local, axis=1), score)
        score_ref[pl.ds(j, half, stride=2), :] = score[:, :nk]
    first = 2 * shards
    tiles = (lines - first) // NPROBE
    nt = probe_ref.shape[2]
    for tile in range(tiles):
        top = fold_sublanes(
            [r_ref[pl.ds(first + rank * tiles + tile, cents, stride=lines), :] for rank in range(NPROBE)]
        )
        four = jnp.concatenate([t[0:1] for t in top], axis=0)
        for i in range(LANES // nt):
            probe_ref[tile * (LANES // nt) + i] = four[:, i * nt : (i + 1) * nt]


def finish(received, shard_index, local_index, shards, cents, nq, nt, nk):
    return pl.pallas_call(
        functools.partial(finish_kernel, shards=shards, cents=cents),
        out_shape=[
            jax.ShapeDtypeStruct((nq, NPROBE, nt), jnp.float32),
            jax.ShapeDtypeStruct((nq, nk), jnp.float32),
        ],
        compiler_params=pltpu.CompilerParams(vmem_limit_bytes=16 * MIB),
        name="finish",
    )(received, shard_index, local_index)


def spread(block, copies):
    return jnp.broadcast_to(block[None], (copies,) + block.shape).reshape((-1,) + block.shape[1:])


def body(queries, centroids, passages, counts, home, candidates):
    nq, nt, dim = queries.shape
    nk = candidates.shape[1]
    shards, cents = lax.axis_size("shard"), lax.axis_size("cent")
    mine = nq // cents
    tokens = queries.reshape(nq * nt, dim)
    own = lax.dynamic_slice_in_dim(tokens, lax.axis_index("cent") * mine * nt, mine * nt, 0)
    gathered = lax.all_to_all(spread(own, shards), "shard", 0, 0, tiled=True)
    blocks = centroids.shape[0] // 4096
    centroids = pltpu.with_memory_space_constraint(centroids, pltpu.HBM)
    lists = probe(tokens, centroids, (), 0, FIRST)
    shard_index, local_index, places, order, tiles = prepare(counts, home, candidates)
    gathered, lists, places, order, tiles = lax.optimization_barrier((gathered, lists, places, order, tiles))
    gathered = pltpu.with_memory_space_constraint(gathered, pltpu.HBM)
    best = maxsim(counts, order, tiles, gathered, passages)
    table = total_scores(best, places, nt)
    table, lists = lax.optimization_barrier((table, lists))
    returned = lax.all_to_all(table, "shard", 0, 0, tiled=True)
    lists = probe(tokens, centroids, (lists,), FIRST, blocks - FIRST)
    final = spread(jnp.concatenate([returned, lists], axis=0), cents)
    received = lax.all_to_all(final, "cent", 0, 0, tiled=True)
    probe_scores, passage_scores = finish(received, shard_index, local_index, shards, cents, nq, nt, nk)
    return jnp.transpose(probe_scores, (0, 2, 1)), passage_scores


def solution(mesh):
    in_specs = (
        P("shard", None, None),
        P("cent", None),
        P("shard", None, None),
        P("shard"),
        P(),
        P("shard", "cent"),
    )
    out_specs = (P("shard", None, None), P("shard", "cent"))
    return jax.shard_map(body, mesh=mesh, in_specs=in_specs, out_specs=out_specs, check_vma=False)
```

```python
import functools

import jax
import jax.numpy as jnp
from jax import lax
from jax.experimental import pallas as pl
from jax.experimental.pallas import tpu as pltpu
from jax.sharding import PartitionSpec as P

NPROBE = 4
LANES = 128
MIB = 1024 * 1024
LEVELS = 3
GROUP = 16
ROWS = 32
PER = 16
FIRST = 5


def insert(running, x):
    out = []
    for rank, held in enumerate(running):
        out.append(jnp.maximum(held, x))
        if rank + 1 < len(running):
            x = jnp.minimum(held, x)
    return out


def streams(levels):
    return [2] * levels + [NPROBE]


def feed(xs, lists):
    for level in range(len(lists) - 1):
        half = len(xs) // 2
        losers = [jnp.minimum(a, b) for a, b in zip(xs[:half], xs[half:])]
        xs = [jnp.maximum(a, b) for a, b in zip(xs[:half], xs[half:])]
        for x in losers:
            lists[level] = insert(lists[level], x)
    for x in xs:
        lists[-1] = insert(lists[-1], x)


def merge_lists(a, b):
    m = [jnp.maximum(a[i], b[NPROBE - 1 - i]) for i in range(NPROBE)]
    for i, j in ((0, 2), (1, 3), (0, 1), (2, 3)):
        m[i], m[j] = jnp.maximum(m[i], m[j]), jnp.minimum(m[i], m[j])
    return m


def fold_sublanes(lists):
    for shift in (4, 2, 1):
        lists = merge_lists(lists, [pltpu.roll(t, shift, 0) for t in lists])
    return lists


def probe_kernel(q_ref, c_ref, *refs):
    before_ref = refs[0] if len(refs) > 2 else None
    o_ref, list_ref = refs[-2:]
    step = pl.program_id(0)
    kept = streams(LEVELS)
    nq = q_ref.shape[0]

    @pl.when(step == 0)
    def _():
        list_ref[...] = jnp.full(list_ref.shape, -jnp.inf, jnp.float32)

    scores = lax.dot_general(
        c_ref[...], q_ref[...], (((1,), (1,)), ((), ())), preferred_element_type=jnp.float32
    )
    for col in range(0, nq, LANES):
        at = 0
        lists = []
        for k in kept:
            lists.append([list_ref[at + a, :, col : col + LANES] for a in range(k)])
            at += k
        for row in range(0, scores.shape[0], 8 * GROUP):
            feed([scores[row + 8 * r : row + 8 * r + 8, col : col + LANES] for r in range(GROUP)], lists)
        at = 0
        for held in lists:
            for a, t in enumerate(held):
                list_ref[at + a, :, col : col + LANES] = t
            at += len(held)

    @pl.when(step == pl.num_programs(0) - 1)
    def _():
        for tile in range(nq // LANES):
            at = 0
            lists = []
            for k in kept:
                lists.append([list_ref[at + a, :, tile * LANES : (tile + 1) * LANES] for a in range(k)])
                at += k
            top = lists[-1]
            for held in lists[:-1]:
                for x in held:
                    top = insert(top, x)
            top = fold_sublanes(top)
            at_rows = [rank * (nq // LANES) + tile for rank in range(NPROBE)]
            top = [t[0:1] for t in top]
            if before_ref is not None:
                top = merge_lists(top, [before_ref[row : row + 1, :] for row in at_rows])
            for rank, row in enumerate(at_rows):
                o_ref[row : row + 1, :] = top[rank]


def probe(queries, centroids, before, first, steps, block=4096):
    nq, dim = queries.shape
    total = steps * block
    rows = NPROBE * nq // LANES
    return pl.pallas_call(
        probe_kernel,
        grid=(steps,),
        in_specs=[
            pl.BlockSpec((nq, dim), lambda i: (0, 0)),
            pl.BlockSpec((block, dim), lambda i: (first + i, 0)),
        ]
        + [pl.BlockSpec((rows, LANES), lambda i: (0, 0))] * len(before),
        out_specs=pl.BlockSpec((rows, LANES), lambda i: (0, 0)),
        out_shape=jax.ShapeDtypeStruct((rows, LANES), jnp.float32),
        scratch_shapes=[pltpu.VMEM((sum(streams(LEVELS)), 8, nq), jnp.float32)],
        compiler_params=pltpu.CompilerParams(vmem_limit_bytes=58 * MIB),
        cost_estimate=pl.CostEstimate(
            flops=4 * nq * total * dim, bytes_accessed=2 * total * dim, transcendentals=0
        ),
        name=f"probe_{first}",
    )(queries, centroids, *before)


def prepare_kernel(count_ref, home_ref, cand_ref, shard_ref, local_ref, place_ref, order_ref, tiles_ref):
    total = count_ref.shape[1]
    counts = jnp.concatenate([count_ref[...], jnp.full((1, LANES - total), 1 - ROWS, jnp.int32)], axis=1)
    tiles = lax.shift_right_arithmetic(counts + (ROWS - 1), ROWS.bit_length() - 1)
    lane = lax.broadcasted_iota(jnp.int32, (LANES, LANES), 1).astype(jnp.float32)
    tiles_across = jnp.broadcast_to(tiles.astype(jnp.float32), (LANES, LANES))
    across = tiles_across * LANES - lane
    down = across.T
    place_across = jnp.sum(jnp.where(down > across, 1.0, 0.0), axis=0, keepdims=True)
    place_down = jnp.sum(jnp.where(across > down, 1.0, 0.0), axis=1, keepdims=True)
    stands = place_down == lane
    order = jnp.sum(jnp.where(stands, lane.T, 0.0), axis=0, keepdims=True)
    sorted_tiles = jnp.sum(jnp.where(stands, tiles_across.T, 0.0), axis=0, keepdims=True)
    place_ref[...] = jnp.broadcast_to(place_across, place_ref.shape).astype(jnp.int32)
    order_ref[...] = order.astype(jnp.int32)
    tiles_ref[...] = sorted_tiles.astype(jnp.int32)
    nq, nk = cand_ref.shape
    cand = jnp.concatenate([cand_ref[...], jnp.zeros((nq, LANES - nk), jnp.int32)], axis=1)
    block, at = lax.shift_right_logical(cand, 7), jnp.bitwise_and(cand, LANES - 1)
    store = jnp.zeros((nq, LANES), jnp.int32)
    for b in range(home_ref.shape[0]):
        line = jnp.broadcast_to(home_ref[b : b + 1, :], (nq, LANES))
        store = jnp.where(block == b, jnp.take_along_axis(line, at, axis=1), store)
    shard_ref[...] = store // total
    local_ref[...] = store % total


def prepare(counts, home, candidates):
    nq = candidates.shape[0]
    index = jax.ShapeDtypeStruct((nq, LANES), jnp.int32)
    line = jax.ShapeDtypeStruct((1, LANES), jnp.int32)
    return pl.pallas_call(
        prepare_kernel,
        out_shape=[index, index, jax.ShapeDtypeStruct((8, LANES), jnp.int32), line, line],
        compiler_params=pltpu.CompilerParams(vmem_limit_bytes=58 * MIB),
        cost_estimate=pl.CostEstimate(flops=10**8, bytes_accessed=10**5, transcendentals=0),
        name="prepare",
    )(counts.reshape(1, -1), home.reshape(-1, LANES), candidates)


def maxsim_kernel(
    count_ref, order_ref, tiles_ref, sent_ref, p_ref, place_ref, o_ref, best_ref, lhs_ref, g_ref, *, width, tokens, mine
):
    count, length, dim = p_ref.shape
    columns = g_ref.shape[0]
    nq = o_ref.shape[0]
    shards, eights = nq // mine, tokens // 8
    for shard in range(shards):
        for k in range(mine * eights):
            to, at_row = (k * shards + shard) * 8, (shard * mine * eights + k) * 8
            g_ref[to : to + 8, :] = sent_ref[at_row : at_row + 8, :]

    def one(g, carry):
        at = pl.multiple_of(g * PER, PER)
        for tiles in range(1, length // ROWS + 1):
            rows = tiles * ROWS

            @pl.when(tiles_ref[0, at] == tiles)
            def _(rows=rows):
                index = lax.broadcasted_iota(jnp.int32, (rows, dim), 0)
                for i in range(PER):
                    p = order_ref[0, at + i]
                    block = p_ref[p, :rows, :].astype(jnp.float32)
                    block = jnp.where(index < count_ref[p], block, block[0:1])
                    lhs_ref[i * rows : (i + 1) * rows, :] = block.astype(lhs_ref.dtype)
                lhs = lhs_ref[: PER * rows, :]
                for col in range(0, columns, width):
                    dots = lax.dot_general(
                        lhs, g_ref[col : col + width, :], (((1,), (1,)), ((), ())), preferred_element_type=jnp.float32
                    )
                    best = jnp.max(dots.reshape(PER, rows // 8, 8, width), axis=1)
                    best_ref[pl.ds(at, PER), col : col + width] = jnp.max(best, axis=1)

        return carry

    lax.fori_loop(0, count // PER, one, 0)
    wide = shards * 8
    rest = jnp.concatenate(
        [sum(best_ref[:, (j * eights + k) * wide : (j * eights + k + 1) * wide] for k in range(eights)) for j in range(mine)],
        axis=1,
    )
    column = lax.broadcasted_iota(jnp.int32, (nq, mine * wide), 1)
    owner = lax.shift_right_logical(column % wide, 3) * mine + column // wide
    pick = (owner == lax.broadcasted_iota(jnp.int32, (nq, mine * wide), 0)).astype(jnp.bfloat16)
    parts = []
    for _ in range(3):
        parts.append(rest.astype(jnp.bfloat16))
        rest = rest - parts[-1].astype(jnp.float32)
    sums = lax.dot_general(
        jnp.concatenate(parts, axis=0), pick, (((1,), (1,)), ((), ())), preferred_element_type=jnp.float32
    )
    sums = sums[:count] + sums[count : 2 * count] + sums[2 * count :]
    sums = jnp.concatenate([sums, jnp.zeros((LANES - count, nq), jnp.float32)], axis=0)
    place = jnp.broadcast_to(place_ref[0:1, :], o_ref.shape)
    o_ref[...] = jnp.take_along_axis(sums.T, place, axis=1)


def maxsim(counts, order, tiles, gathered, passages, places, tokens, mine, width=512):
    columns, dim = gathered.shape
    count, length, _ = passages.shape
    nq = columns // tokens
    vmem = pl.BlockSpec(memory_space=pltpu.VMEM)
    smem = pl.BlockSpec(memory_space=pltpu.SMEM)
    return pl.pallas_call(
        functools.partial(maxsim_kernel, width=width, tokens=tokens, mine=mine),
        in_specs=[smem, smem, smem, vmem, vmem, vmem],
        out_specs=vmem,
        out_shape=jax.ShapeDtypeStruct((nq, LANES), jnp.float32),
        scratch_shapes=[
            pltpu.VMEM((count, columns), jnp.float32),
            pltpu.VMEM((PER * length, dim), jnp.bfloat16),
            pltpu.VMEM(gathered.shape, gathered.dtype),
        ],
        compiler_params=pltpu.CompilerParams(vmem_limit_bytes=40 * MIB),
        cost_estimate=pl.CostEstimate(
            flops=2 * columns * count * length * dim, bytes_accessed=2 * passages.size, transcendentals=0
        ),
        name="maxsim",
    )(counts, order, tiles, gathered, passages, places)


def finish_kernel(r_ref, shard_ref, local_ref, probe_ref, score_ref, *, shards, cents):
    lines = r_ref.shape[0] // cents
    half = shard_ref.shape[0] // 2
    nk = score_ref.shape[1]
    for j in range(2):
        home = shard_ref[pl.ds(j, half, stride=2), :]
        local = local_ref[pl.ds(j, half, stride=2), :]
        score = jnp.zeros(home.shape, jnp.float32)
        for s in range(shards):
            table = r_ref[pl.ds(2 * s + j, cents, stride=lines), :]
            score = jnp.where(home == s, jnp.take_along_axis(table, local, axis=1), score)
        score_ref[pl.ds(j, half, stride=2), :] = score[:, :nk]
    first = 2 * shards
    tiles = (lines - first) // NPROBE
    nt = probe_ref.shape[2]
    for tile in range(tiles):
        top = fold_sublanes(
            [r_ref[pl.ds(first + rank * tiles + tile, cents, stride=lines), :] for rank in range(NPROBE)]
        )
        four = jnp.concatenate([t[0:1] for t in top], axis=0)
        for i in range(LANES // nt):
            probe_ref[tile * (LANES // nt) + i] = four[:, i * nt : (i + 1) * nt]


def finish(received, shard_index, local_index, shards, cents, nq, nt, nk):
    return pl.pallas_call(
        functools.partial(finish_kernel, shards=shards, cents=cents),
        out_shape=[
            jax.ShapeDtypeStruct((nq, NPROBE, nt), jnp.float32),
            jax.ShapeDtypeStruct((nq, nk), jnp.float32),
        ],
        compiler_params=pltpu.CompilerParams(vmem_limit_bytes=16 * MIB),
        name="finish",
    )(received, shard_index, local_index)


def spread(block, copies):
    return jnp.broadcast_to(block[None], (copies,) + block.shape).reshape((-1,) + block.shape[1:])


def body(queries, centroids, passages, counts, home, candidates):
    nq, nt, dim = queries.shape
    nk = candidates.shape[1]
    shards, cents = lax.axis_size("shard"), lax.axis_size("cent")
    mine = nq // cents
    tokens = queries.reshape(nq * nt, dim)
    own = lax.dynamic_slice_in_dim(tokens, lax.axis_index("cent") * mine * nt, mine * nt, 0)
    gathered = lax.all_to_all(spread(own, shards), "shard", 0, 0, tiled=True)
    blocks = centroids.shape[0] // 4096
    centroids = pltpu.with_memory_space_constraint(centroids, pltpu.HBM)
    lists = probe(tokens, centroids, (), 0, FIRST)
    shard_index, local_index, places, order, tiles = prepare(counts, home, candidates)
    gathered, lists, places, order, tiles = lax.optimization_barrier((gathered, lists, places, order, tiles))
    gathered = pltpu.with_memory_space_constraint(gathered, pltpu.HBM)
    table = maxsim(counts, order, tiles, gathered, passages, places, nt, mine)
    table, lists = lax.optimization_barrier((table, lists))
    returned = lax.all_to_all(table, "shard", 0, 0, tiled=True)
    lists = probe(tokens, centroids, (lists,), FIRST, blocks - FIRST)
    final = spread(jnp.concatenate([returned, lists], axis=0), cents)
    received = lax.all_to_all(final, "cent", 0, 0, tiled=True)
    probe_scores, passage_scores = finish(received, shard_index, local_index, shards, cents, nq, nt, nk)
    return jnp.transpose(probe_scores, (0, 2, 1)), passage_scores


def solution(mesh):
    in_specs = (
        P("shard", None, None),
        P("cent", None),
        P("shard", None, None),
        P("shard"),
        P(),
        P("shard", "cent"),
    )
    out_specs = (P("shard", None, None), P("shard", "cent"))
    return jax.shard_map(body, mesh=mesh, in_specs=in_specs, out_specs=out_specs, check_vma=False)
```

```python
import functools

import jax
import jax.numpy as jnp
from jax import lax
from jax.experimental import pallas as pl
from jax.experimental.pallas import tpu as pltpu
from jax.sharding import PartitionSpec as P

NPROBE = 4
LANES = 128
MIB = 1024 * 1024
LEVELS = 3
GROUP = 16
ROWS = 32
PER = 16
FIRST = 6


def insert(running, x):
    out = []
    for rank, held in enumerate(running):
        out.append(jnp.maximum(held, x))
        if rank + 1 < len(running):
            x = jnp.minimum(held, x)
    return out


def streams(levels):
    return [2] * levels + [NPROBE]


def feed(xs, lists):
    for level in range(len(lists) - 1):
        half = len(xs) // 2
        losers = [jnp.minimum(a, b) for a, b in zip(xs[:half], xs[half:])]
        xs = [jnp.maximum(a, b) for a, b in zip(xs[:half], xs[half:])]
        for x in losers:
            lists[level] = insert(lists[level], x)
    for x in xs:
        lists[-1] = insert(lists[-1], x)


def merge_lists(a, b):
    m = [jnp.maximum(a[i], b[NPROBE - 1 - i]) for i in range(NPROBE)]
    for i, j in ((0, 2), (1, 3), (0, 1), (2, 3)):
        m[i], m[j] = jnp.maximum(m[i], m[j]), jnp.minimum(m[i], m[j])
    return m


def fold_sublanes(lists):
    for shift in (4, 2, 1):
        lists = merge_lists(lists, [pltpu.roll(t, shift, 0) for t in lists])
    return lists


def probe_kernel(q_ref, c_ref, *refs):
    before_ref = refs[0] if len(refs) > 2 else None
    o_ref, list_ref = refs[-2:]
    step = pl.program_id(0)
    kept = streams(LEVELS)
    nq = q_ref.shape[0]

    @pl.when(step == 0)
    def _():
        list_ref[...] = jnp.full(list_ref.shape, -jnp.inf, jnp.float32)

    scores = lax.dot_general(
        c_ref[...], q_ref[...], (((1,), (1,)), ((), ())), preferred_element_type=jnp.float32
    )
    for col in range(0, nq, LANES):
        at = 0
        lists = []
        for k in kept:
            lists.append([list_ref[at + a, :, col : col + LANES] for a in range(k)])
            at += k
        for row in range(0, scores.shape[0], 8 * GROUP):
            feed([scores[row + 8 * r : row + 8 * r + 8, col : col + LANES] for r in range(GROUP)], lists)
        at = 0
        for held in lists:
            for a, t in enumerate(held):
                list_ref[at + a, :, col : col + LANES] = t
            at += len(held)

    @pl.when(step == pl.num_programs(0) - 1)
    def _():
        for tile in range(nq // LANES):
            at = 0
            lists = []
            for k in kept:
                lists.append([list_ref[at + a, :, tile * LANES : (tile + 1) * LANES] for a in range(k)])
                at += k
            top = lists[-1]
            for held in lists[:-1]:
                for x in held:
                    top = insert(top, x)
            top = fold_sublanes(top)
            at_rows = [rank * (nq // LANES) + tile for rank in range(NPROBE)]
            top = [t[0:1] for t in top]
            if before_ref is not None:
                top = merge_lists(top, [before_ref[row : row + 1, :] for row in at_rows])
            for rank, row in enumerate(at_rows):
                o_ref[row : row + 1, :] = top[rank]


def probe(queries, centroids, before, first, steps, block=4096):
    nq, dim = queries.shape
    total = steps * block
    rows = NPROBE * nq // LANES
    return pl.pallas_call(
        probe_kernel,
        grid=(steps,),
        in_specs=[
            pl.BlockSpec((nq, dim), lambda i: (0, 0)),
            pl.BlockSpec((block, dim), lambda i: (first + i, 0)),
        ]
        + [pl.BlockSpec((rows, LANES), lambda i: (0, 0))] * len(before),
        out_specs=pl.BlockSpec((rows, LANES), lambda i: (0, 0)),
        out_shape=jax.ShapeDtypeStruct((rows, LANES), jnp.float32),
        scratch_shapes=[pltpu.VMEM((sum(streams(LEVELS)), 8, nq), jnp.float32)],
        compiler_params=pltpu.CompilerParams(vmem_limit_bytes=58 * MIB),
        cost_estimate=pl.CostEstimate(
            flops=4 * nq * total * dim, bytes_accessed=2 * total * dim, transcendentals=0
        ),
        name=f"probe_{first}",
    )(queries, centroids, *before)


def prepare_kernel(count_ref, home_ref, cand_ref, shard_ref, local_ref, place_ref, order_ref, tiles_ref):
    total = count_ref.shape[1]
    counts = jnp.concatenate([count_ref[...], jnp.full((1, LANES - total), 1 - ROWS, jnp.int32)], axis=1)
    tiles = lax.shift_right_arithmetic(counts + (ROWS - 1), ROWS.bit_length() - 1)
    lane = lax.broadcasted_iota(jnp.int32, (LANES, LANES), 1).astype(jnp.float32)
    tiles_across = jnp.broadcast_to(tiles.astype(jnp.float32), (LANES, LANES))
    across = tiles_across * LANES - lane
    down = across.T
    place_across = jnp.sum(jnp.where(down > across, 1.0, 0.0), axis=0, keepdims=True)
    place_down = jnp.sum(jnp.where(across > down, 1.0, 0.0), axis=1, keepdims=True)
    stands = place_down == lane
    order = jnp.sum(jnp.where(stands, lane.T, 0.0), axis=0, keepdims=True)
    sorted_tiles = jnp.sum(jnp.where(stands, tiles_across.T, 0.0), axis=0, keepdims=True)
    place_ref[...] = jnp.broadcast_to(place_across, place_ref.shape).astype(jnp.int32)
    order_ref[...] = order.astype(jnp.int32)
    tiles_ref[...] = sorted_tiles.astype(jnp.int32)
    nq, nk = cand_ref.shape
    cand = jnp.concatenate([cand_ref[...], jnp.zeros((nq, LANES - nk), jnp.int32)], axis=1)
    block, at = lax.shift_right_logical(cand, 7), jnp.bitwise_and(cand, LANES - 1)
    store = jnp.zeros((nq, LANES), jnp.int32)
    for b in range(home_ref.shape[0]):
        line = jnp.broadcast_to(home_ref[b : b + 1, :], (nq, LANES))
        store = jnp.where(block == b, jnp.take_along_axis(line, at, axis=1), store)
    shard_ref[...] = store // total
    local_ref[...] = store % total


def prepare(counts, home, candidates):
    nq = candidates.shape[0]
    index = jax.ShapeDtypeStruct((nq, LANES), jnp.int32)
    line = jax.ShapeDtypeStruct((1, LANES), jnp.int32)
    return pl.pallas_call(
        prepare_kernel,
        out_shape=[index, index, jax.ShapeDtypeStruct((8, LANES), jnp.int32), line, line],
        compiler_params=pltpu.CompilerParams(vmem_limit_bytes=58 * MIB),
        cost_estimate=pl.CostEstimate(flops=10**8, bytes_accessed=10**5, transcendentals=0),
        name="prepare",
    )(counts.reshape(1, -1), home.reshape(-1, LANES), candidates)


def maxsim_kernel(
    count_ref, order_ref, tiles_ref, sent_ref, p_ref, place_ref, o_ref, best_ref, lhs_ref, g_ref, *, width, tokens, mine
):
    count, length, dim = p_ref.shape
    columns = g_ref.shape[0]
    nq = o_ref.shape[0]
    shards, eights = nq // mine, tokens // 8
    for shard in range(shards):
        for k in range(mine * eights):
            to, at_row = (k * shards + shard) * 8, (shard * mine * eights + k) * 8
            g_ref[to : to + 8, :] = sent_ref[at_row : at_row + 8, :]

    def one(g, carry):
        at = pl.multiple_of(g * PER, PER)
        for tiles in range(1, length // ROWS + 1):
            rows = tiles * ROWS

            @pl.when(tiles_ref[0, at] == tiles)
            def _(rows=rows):
                index = lax.broadcasted_iota(jnp.int32, (rows, dim), 0)
                for i in range(PER):
                    p = order_ref[0, at + i]
                    block = p_ref[p, :rows, :].astype(jnp.float32)
                    block = jnp.where(index < count_ref[p], block, block[0:1])
                    lhs_ref[i * rows : (i + 1) * rows, :] = block.astype(lhs_ref.dtype)
                lhs = lhs_ref[: PER * rows, :]
                for col in range(0, columns, width):
                    dots = lax.dot_general(
                        lhs, g_ref[col : col + width, :], (((1,), (1,)), ((), ())), preferred_element_type=jnp.float32
                    )
                    best = jnp.max(dots.reshape(PER, rows // 8, 8, width), axis=1)
                    best_ref[pl.ds(at, PER), col : col + width] = jnp.max(best, axis=1)

        return carry

    lax.fori_loop(0, count // PER, one, 0)
    wide = shards * 8
    rest = jnp.concatenate(
        [sum(best_ref[:, (j * eights + k) * wide : (j * eights + k + 1) * wide] for k in range(eights)) for j in range(mine)],
        axis=1,
    )
    column = lax.broadcasted_iota(jnp.int32, (nq, mine * wide), 1)
    owner = lax.shift_right_logical(column % wide, 3) * mine + column // wide
    pick = (owner == lax.broadcasted_iota(jnp.int32, (nq, mine * wide), 0)).astype(jnp.bfloat16)
    parts = []
    for _ in range(3):
        parts.append(rest.astype(jnp.bfloat16))
        rest = rest - parts[-1].astype(jnp.float32)
    sums = lax.dot_general(
        jnp.concatenate(parts, axis=0), pick, (((1,), (1,)), ((), ())), preferred_element_type=jnp.float32
    )
    sums = sums[:count] + sums[count : 2 * count] + sums[2 * count :]
    sums = jnp.concatenate([sums, jnp.zeros((LANES - count, nq), jnp.float32)], axis=0)
    place = jnp.broadcast_to(place_ref[0:1, :], o_ref.shape)
    o_ref[...] = jnp.take_along_axis(sums.T, place, axis=1)


def maxsim(counts, order, tiles, gathered, passages, places, tokens, mine, width=512):
    columns, dim = gathered.shape
    count, length, _ = passages.shape
    nq = columns // tokens
    vmem = pl.BlockSpec(memory_space=pltpu.VMEM)
    smem = pl.BlockSpec(memory_space=pltpu.SMEM)
    return pl.pallas_call(
        functools.partial(maxsim_kernel, width=width, tokens=tokens, mine=mine),
        in_specs=[smem, smem, smem, vmem, vmem, vmem],
        out_specs=vmem,
        out_shape=jax.ShapeDtypeStruct((nq, LANES), jnp.float32),
        scratch_shapes=[
            pltpu.VMEM((count, columns), jnp.float32),
            pltpu.VMEM((PER * length, dim), jnp.bfloat16),
            pltpu.VMEM(gathered.shape, gathered.dtype),
        ],
        compiler_params=pltpu.CompilerParams(vmem_limit_bytes=40 * MIB),
        cost_estimate=pl.CostEstimate(
            flops=2 * columns * count * length * dim, bytes_accessed=2 * passages.size, transcendentals=0
        ),
        name="maxsim",
    )(counts, order, tiles, gathered, passages, places)


def finish_kernel(r_ref, shard_ref, local_ref, probe_ref, score_ref, *, shards, cents):
    lines = r_ref.shape[0] // cents
    half = shard_ref.shape[0] // 2
    nk = score_ref.shape[1]
    for j in range(2):
        home = shard_ref[pl.ds(j, half, stride=2), :]
        local = local_ref[pl.ds(j, half, stride=2), :]
        score = jnp.zeros(home.shape, jnp.float32)
        for s in range(shards):
            table = r_ref[pl.ds(2 * s + j, cents, stride=lines), :]
            score = jnp.where(home == s, jnp.take_along_axis(table, local, axis=1), score)
        score_ref[pl.ds(j, half, stride=2), :] = score[:, :nk]
    first = 2 * shards
    tiles = (lines - first) // NPROBE
    nt = probe_ref.shape[2]
    for tile in range(tiles):
        top = fold_sublanes(
            [r_ref[pl.ds(first + rank * tiles + tile, cents, stride=lines), :] for rank in range(NPROBE)]
        )
        four = jnp.concatenate([t[0:1] for t in top], axis=0)
        for i in range(LANES // nt):
            probe_ref[tile * (LANES // nt) + i] = four[:, i * nt : (i + 1) * nt]


def finish(received, shard_index, local_index, shards, cents, nq, nt, nk):
    return pl.pallas_call(
        functools.partial(finish_kernel, shards=shards, cents=cents),
        out_shape=[
            jax.ShapeDtypeStruct((nq, NPROBE, nt), jnp.float32),
            jax.ShapeDtypeStruct((nq, nk), jnp.float32),
        ],
        compiler_params=pltpu.CompilerParams(vmem_limit_bytes=16 * MIB),
        name="finish",
    )(received, shard_index, local_index)


def spread(block, copies):
    return jnp.broadcast_to(block[None], (copies,) + block.shape).reshape((-1,) + block.shape[1:])


def body(queries, centroids, passages, counts, home, candidates):
    nq, nt, dim = queries.shape
    nk = candidates.shape[1]
    shards, cents = lax.axis_size("shard"), lax.axis_size("cent")
    mine = nq // cents
    tokens = queries.reshape(nq * nt, dim)
    own = lax.dynamic_slice_in_dim(tokens, lax.axis_index("cent") * mine * nt, mine * nt, 0)
    gathered = lax.all_to_all(spread(own, shards), "shard", 0, 0, tiled=True)
    blocks = centroids.shape[0] // 4096
    centroids = pltpu.with_memory_space_constraint(centroids, pltpu.HBM)
    lists = probe(tokens, centroids, (), 0, FIRST)
    shard_index, local_index, places, order, tiles = prepare(counts, home, candidates)
    gathered, lists, places, order, tiles = lax.optimization_barrier((gathered, lists, places, order, tiles))
    gathered = pltpu.with_memory_space_constraint(gathered, pltpu.HBM)
    table = maxsim(counts, order, tiles, gathered, passages, places, nt, mine)
    table, lists = lax.optimization_barrier((table, lists))
    returned = lax.all_to_all(table, "shard", 0, 0, tiled=True)
    lists = probe(tokens, centroids, (lists,), FIRST, blocks - FIRST)
    final = spread(jnp.concatenate([returned, lists], axis=0), cents)
    received = lax.all_to_all(final, "cent", 0, 0, tiled=True)
    probe_scores, passage_scores = finish(received, shard_index, local_index, shards, cents, nq, nt, nk)
    return jnp.transpose(probe_scores, (0, 2, 1)), passage_scores


def solution(mesh):
    in_specs = (
        P("shard", None, None),
        P("cent", None),
        P("shard", None, None),
        P("shard"),
        P(),
        P("shard", "cent"),
    )
    out_specs = (P("shard", None, None), P("shard", "cent"))
    return jax.shard_map(body, mesh=mesh, in_specs=in_specs, out_specs=out_specs, check_vma=False)
```
